32 devices in a mesh: dp: 8 (over z, y), tp: 4 (over x, core).
Axes of the slice: x: 2, y: 2, z: 4, core: 2. Of those that a mesh axis runs over, the one named last changes fastest.
Arguments:
- tokens: bfloat16 [16384, 768], P(('dp', 'tp')), may hold values from -6 to 6
- prompt: bfloat16 [50, 768], replicated, may hold values from -6 to 6
- qkv_weight: bfloat16 [768, 3, 768], P('dp', None, 'tp'), may hold values from -0.21875 to 0.21875
- out_weight: bfloat16 [768, 768], P('tp', 'dp'), may hold values from -1.75 to 1.75
- up_weight: bfloat16 [768, 3072], P('dp', 'tp'), may hold values from -0.21875 to 0.21875
- down_weight: bfloat16 [3072, 768], P('tp', 'dp'), may hold values from -0.109375 to 0.109375
- gain_one: bfloat16 [768], replicated, may hold values from 0.5 to 1.5
- gain_two: bfloat16 [768], replicated, may hold values from 0.5 to 1.5
- segment_ids: int32 [16, 1024], P('dp'), may hold values from 0 to 3, as said below
- pad_flags: int32 [16, 1024], P('dp'), may hold values from 0 to 1, as said below
- cotangent: bfloat16 [16384, 768], P(('dp', 'tp')), may hold values from -6 to 6
Outputs:
- output: bfloat16 [16384, 768], P(('dp', 'tp'))
- grad_tokens: bfloat16 [16384, 768], P(('dp', 'tp'))
- grad_prompt: bfloat16 [50, 768], replicated
The draws below stay inside these ranges and needn't reach their ends.
Inputs may be any that keep to these rules, and one draw needn't show every extreme that they name: `segment_ids`: each row holds 4 images of 247 consecutive tokens with ids 0 to 3 in order; a padding token carries the id of the image before it, or 0 before the first image. `pad_flags`: 1 exactly on the 36 tokens of each row that belong to no image.
All inputs are finite; a program needn't handle non-finite values.
Results may differ from the reference program's by a relative error of at most 0.018.
Values may be sent and summed in bfloat16 or wider, within the bound.
No kernel may reach another device: no remote copies, remote signals or barrier semaphores. Data moves between devices by JAX's collectives and lax.ppermute only.
A program may use at most 128 MiB of HBM per device.

```python
import math
import jax
import jax.numpy as jnp
from jax import lax

D = 768
HEADS = 12
HD = 64
FF = 3072
PROMPTS = 50
IMG = 247
NIMG = 4
SEQ = 1024
ROWS = 16
TOKENS = 16384


def row_layout(key):
    spare = SEQ - NIMG * IMG
    cuts = jnp.sort(jax.random.randint(jax.random.fold_in(key, 11), (ROWS, NIMG), 0, spare + 1), axis=-1)
    starts = cuts + jnp.arange(NIMG, dtype=jnp.int32)[None, :] * IMG
    positions = jnp.arange(SEQ, dtype=jnp.int32)
    began = positions[None, :, None] >= starts[:, None, :]
    segment = jnp.maximum(jnp.sum(began.astype(jnp.int32), axis=-1) - 1, 0)
    inside = began & (positions[None, :, None] < starts[:, None, :] + IMG)
    padding = 1 - jnp.sum(inside.astype(jnp.int32), axis=-1)
    return (segment.astype(jnp.int32), padding.astype(jnp.int32))


def draw_segment_ids(key, part):
    return row_layout(key)[0]


def draw_pad_flags(key, part):
    return row_layout(key)[1]


def block_scale(stream_key, dims, split, least, top_value):
    loudness = 1.0
    for position, parts in split:
        steps = jax.random.uniform(jax.random.fold_in(jax.random.fold_in(stream_key, 6), position), (parts,), jnp.float32, least / len(split), top_value / len(split))
        loudness = loudness * jnp.repeat(jnp.exp(steps), dims[position] // parts).reshape((-1,) + (1,) * (len(dims) - 1 - position))
    return loudness


def gaussian(stream_key, shape, width, most, cuts=(), held_as=jnp.bfloat16):
    entries = width * jax.random.normal(stream_key, shape, jnp.float32)
    if cuts:
        entries = entries * block_scale(stream_key, shape, cuts, -0.22, 0.18)
    return jnp.clip(entries, -most, most).astype(held_as)


def setup_inputs(seed: int = 0) -> dict:
    splits = jax.random.split(jax.random.key(seed), 12)
    tokens = gaussian(splits[0], (TOKENS, D), 1.0, 6.0, ((0, 32),))
    prompt = gaussian(splits[1], (PROMPTS, D), 1.0, 6.0)
    qkv_weight = gaussian(splits[2], (D, 3, D), D ** -0.5, 0.21875, ((0, 8), (2, 4)))
    out_weight = gaussian(splits[3], (D, D), (D // 64) ** -0.5, 1.75, ((0, 4), (1, 8)))
    up_weight = gaussian(splits[4], (D, FF), D ** -0.5, 0.21875, ((0, 8), (1, 4)))
    down_weight = gaussian(splits[5], (FF, D), FF ** -0.5, 0.109375, ((0, 4), (1, 8)))
    gain_one = jnp.clip(1.0 + 0.1 * jax.random.normal(splits[6], (D,), jnp.float32), 0.5, 1.5).astype(jnp.bfloat16)
    gain_two = jnp.clip(1.0 + 0.1 * jax.random.normal(splits[7], (D,), jnp.float32), 0.5, 1.5).astype(jnp.bfloat16)
    segment_ids = draw_segment_ids(jax.random.fold_in(splits[11], 71), 0)
    pad_flags = draw_pad_flags(jax.random.fold_in(splits[11], 71), 0)
    cotangent = gaussian(splits[10], (TOKENS, D), 1.0, 6.0, ((0, 32),))
    return {"tokens": tokens, "prompt": prompt, "qkv_weight": qkv_weight, "out_weight": out_weight, "up_weight": up_weight, "down_weight": down_weight, "gain_one": gain_one, "gain_two": gain_two, "segment_ids": segment_ids, "pad_flags": pad_flags, "cotangent": cotangent}


@jax.custom_vjp
def low(v):
    return lax.optimization_barrier(v.astype(jnp.bfloat16)).astype(jnp.float32)

@jax.custom_vjp
def low_back(v):
    return v

def low_keep(v):
    return (low(v), None)

def low_pass(kept, grad):
    return (grad,)

def back_keep(v):
    return (v, None)

def back_low(kept, grad):
    return (low(grad),)
low.defvjp(low_keep, low_pass)
low_back.defvjp(back_keep, back_low)
norm_eps = 1e-06
neg_fill = -1e+30
highest = lax.Precision.HIGHEST

def layer_norm(values, gain):
    centre = lax.optimization_barrier(jnp.mean(values, axis=-1, keepdims=True))
    centred = values - centre
    spread = lax.optimization_barrier(jnp.mean(centred * centred, axis=-1, keepdims=True))
    return centred * lax.rsqrt(spread + norm_eps) * gain

def prompt_layout(segment_ids, pad_flags):
    seq_len = segment_ids.shape[1]
    positions = jnp.arange(seq_len, dtype=jnp.int32)
    images = jnp.arange(NIMG, dtype=jnp.int32)
    live = pad_flags == 0
    same_image = segment_ids[:, :, None] == images[None, None, :]
    starts = lax.optimization_barrier(jnp.min(jnp.where(same_image & live[:, :, None], positions[None, :, None], seq_len), axis=1))
    own_start = lax.optimization_barrier(jnp.sum(jnp.where(same_image, starts[:, None, :], 0), axis=-1))
    offset = positions[None, :] - own_start
    chosen = live & (offset >= 1) & (offset <= PROMPTS)
    return jnp.where(chosen, offset - 1, -1).astype(jnp.int32)

def attend_row(packed):
    qkv_row, seg_row, pad_row = packed
    queries = qkv_row[:, 0]
    keys_all = qkv_row[:, 1]
    values_all = qkv_row[:, 2]
    scale = 1.0 / math.sqrt(HD)
    scores = low_back(scale * jnp.einsum('qhd,khd->hqk', queries, keys_all, precision=highest))
    allowed = (seg_row[:, None] == seg_row[None, :]) & (pad_row[None, :] == 0)
    scores = jnp.where(allowed[None], scores, neg_fill)
    top = lax.optimization_barrier(jnp.max(scores, axis=-1, keepdims=True))
    weights = jnp.exp(scores - top)
    probs = low(weights / lax.optimization_barrier(jnp.sum(weights, axis=-1, keepdims=True)))
    return low_back(low(jnp.einsum('hqk,khd->qhd', probs, values_all, precision=highest)))

def reference(tokens, prompt, qkv_weight, out_weight, up_weight, down_weight, gain_one, gain_two, segment_ids, pad_flags, cotangent):
    index = prompt_layout(segment_ids, pad_flags).reshape(-1)
    table_index = jnp.clip(index, 0, PROMPTS - 1)
    chosen = (index >= 0)[:, None]
    qkv_matrix = qkv_weight.astype(jnp.float32).reshape(D, 3 * D)
    out_matrix = out_weight.astype(jnp.float32)
    up_matrix = up_weight.astype(jnp.float32)
    down_matrix = down_weight.astype(jnp.float32)
    first_gain = gain_one.astype(jnp.float32)
    second_gain = gain_two.astype(jnp.float32)
    attend_whole = jax.checkpoint(attend_row)

    def forward(token_values, prompt_values):
        start = jnp.where(chosen, prompt_values[table_index], token_values)
        normed = low(layer_norm(start, first_gain))
        qkv = low_back(low(jnp.dot(normed, qkv_matrix, precision=highest)))
        qkv = qkv.reshape(ROWS, SEQ, 3, HEADS, HD)
        mixed = lax.map(attend_whole, (qkv, segment_ids, pad_flags)).reshape(ROWS * SEQ, D)
        branch = low_back(jnp.dot(mixed, out_matrix, precision=highest))
        after_attn = start + branch
        normed_two = low(layer_norm(after_attn, second_gain))
        pre = low_back(jnp.dot(normed_two, up_matrix, precision=highest))
        act = low(jax.nn.gelu(pre, approximate=False))
        branch_two = low_back(jnp.dot(act, down_matrix, precision=highest))
        return after_attn + branch_two
    output, pull = jax.vjp(forward, tokens.astype(jnp.float32), prompt.astype(jnp.float32))
    grad_tok, grad_prm = pull(cotangent.astype(jnp.float32))
    return (output.astype(jnp.bfloat16), grad_tok.astype(jnp.bfloat16), (grad_prm / ROWS).astype(jnp.bfloat16))
```

```python
import functools

import jax
import jax.numpy as jnp
from jax import lax
from jax.experimental import pallas as pl
from jax.experimental.pallas import tpu as pltpu
from jax.sharding import PartitionSpec as P

HD = 64
PROMPTS = 50
HALO = 32
WIN = 304
NT = (((1,), (1,)), ((), ()))
NN = (((1,), (0,)), ((), ()))
TN = (((0,), (0,)), ((), ()))
eps = 1e-6
fill = -1e30
floor = -1e29
bf16 = jnp.bfloat16
f32 = jnp.float32


def dot(a, b, dims=NN):
    return lax.dot_general(a, b, dims, preferred_element_type=f32)


def norm_parts(values):
    centred = values - jnp.mean(values, axis=-1, keepdims=True)
    scale = lax.rsqrt(jnp.mean(centred * centred, axis=-1, keepdims=True) + eps)
    return centred * scale, scale


def norm_back(unit, scale, grad, gain):
    u = grad * gain
    return scale * (
        u - jnp.mean(u, axis=-1, keepdims=True) - unit * jnp.mean(u * unit, axis=-1, keepdims=True)
    )


def window_starts(count):
    return (0, count - WIN)


def join_windows(first, second, count):
    low = count - WIN
    return jnp.concatenate([first[:low], first[low:] + second[: WIN - low], second[WIN - low :]], 0)


def fetch(plan, offs, refs, buf, sems):
    for block, copies in enumerate(plan):
        for which, source, rows, slot in copies:
            pltpu.make_async_copy(
                refs[which].at[pl.ds(source, rows)],
                buf.at[block, pl.ds(pl.multiple_of(offs[slot], 16), rows)],
                sems.at[block],
            ).start()


def arrive(buf, sems, block):
    pltpu.make_async_copy(buf.at[block], buf.at[block], sems.at[block]).wait()


def enter_kernel(place, own, own_halo, cot, cot_halo, prompt, index, gain, start, normed, cot_out):
    main = pl.multiple_of(place[0], HALO)
    side = pl.multiple_of(place[1], HALO)
    rows = own.shape[0]
    start[pl.ds(main, rows), :] = own[...]
    start[pl.ds(side, HALO), :] = own_halo[...]
    cot_out[pl.ds(main, rows), :] = cot[...]
    cot_out[pl.ds(side, HALO), :] = cot_halo[...]
    idx = index[...]
    lanes = lax.broadcasted_iota(jnp.int32, (idx.shape[0], PROMPTS), 1)
    onehot = (idx == lanes).astype(f32).astype(bf16)
    picked = dot(onehot, prompt[...])
    value = jnp.where(idx >= 0, picked, start[...].astype(f32))
    start[...] = value.astype(bf16)
    unit, _ = norm_parts(value)
    normed[...] = (unit * gain[...].astype(f32)).astype(bf16)


def attend_kernel(plan, offs, normed, start, gain, qseg, krow_a, krow_b, *rest):
    n = len(rest) - 7
    refs, (after, normed_two, qkv_out, buf, bias, mix, sems) = rest[:n], rest[n:]
    count = normed.shape[0]
    width = qkv_out.shape[2]
    heads = width // (3 * HD)
    inner = heads * HD
    fetch(plan, offs, refs, buf, sems)
    starts = window_starts(count)
    for s, krow in enumerate((krow_a, krow_b)):
        bias[s] = jnp.where(
            qseg[starts[s] : starts[s] + WIN, :] == krow[:, starts[s] : starts[s] + WIN]
            if s == 0
            else qseg[starts[s] : starts[s] + WIN, :] == krow[...][:, starts[s] : starts[s] + WIN],
            0.0,
            fill,
        )
    after[...] = start[...].astype(f32)

    def step(block, carry):
        arrive(buf, sems, block)
        weight = buf.at[block]
        qkv = dot(normed[...], weight[:, :width]).astype(bf16)
        qkv_out[block] = qkv
        for h in range(heads):
            parts = []
            for s in range(2):
                rows = slice(starts[s], starts[s] + WIN)
                q = qkv[rows, h * HD : (h + 1) * HD] * bf16(HD**-0.5)
                k = qkv[rows, inner + h * HD : inner + (h + 1) * HD]
                v = qkv[rows, 2 * inner + h * HD : 2 * inner + (h + 1) * HD]
                scores = dot(q, k, NT) + bias[s]
                top = jnp.maximum(jnp.max(scores, axis=-1, keepdims=True), floor)
                weights = jnp.exp(scores - top)
                total = jnp.maximum(jnp.sum(weights, axis=-1, keepdims=True), 1e-30)
                probs = (weights * (1.0 / total)).astype(bf16)
                parts.append(dot(probs, v))
            mix[:, h * HD : (h + 1) * HD] = join_windows(parts[0], parts[1], count).astype(bf16)
        after[...] += dot(mix[...], weight[:, width:], NT)
        return carry

    lax.fori_loop(0, buf.shape[0], step, 0)
    unit, _ = norm_parts(after[...])
    normed_two[...] = (unit * gain[...].astype(f32)).astype(bf16)


def mlp_kernel(plan, offs, normed_two, cot, after, gain, *rest):
    n = len(rest) - 8
    refs, (output, grad_after, branch, up, down, total, gsum, sems) = rest[:n], rest[n:]
    half = n // 2
    fetch(plan, offs, refs[:half], up, sems.at[0])
    fetch(plan, offs, refs[half:], down, sems.at[1])
    total[...] = after[...]
    gsum[...] = jnp.zeros_like(gsum)

    def step(block, carry):
        arrive(up, sems.at[0], block)
        arrive(down, sems.at[1], block)
        pre = dot(normed_two[...], up[block])
        cdf = 0.5 + 0.5 * lax.erf(pre * (0.5**0.5))
        slope = cdf + pre * (jnp.exp(-0.5 * pre * pre) * 0.3989422804014327)
        act = (pre * cdf).astype(bf16)
        back = dot(cot[...], down[block])
        grad_pre = (back * slope).astype(bf16)
        total[...] += dot(act, down[block], NT)
        gsum[...] += dot(grad_pre, up[block], NT)
        return carry

    lax.fori_loop(0, up.shape[0], step, 0)
    output[...] = total[...].astype(bf16)
    unit, scale = norm_parts(after[...])
    grad = cot[...].astype(f32) + norm_back(unit, scale, gsum[...], gain[...].astype(f32))
    grad_after[...] = grad
    branch[...] = grad.astype(bf16)


def back_kernel(plan, offs, branch, grad_after, start, qkv_all, gain, qrow, kcol_a, kcol_b, index, *rest):
    n = len(rest) - 8
    refs, (grad_tok, grad_prm, buf, bias, gmix, gqkv, gsum, sems) = rest[:n], rest[n:]
    count = branch.shape[0]
    width = qkv_all.shape[2]
    heads = width // (3 * HD)
    inner = heads * HD
    fetch(plan, offs, refs, buf, sems)
    starts = window_starts(count)
    for s, kcol in enumerate((kcol_a, kcol_b)):
        bias[s] = jnp.where(
            kcol[starts[s] : starts[s] + WIN, :] == qrow[...][:, starts[s] : starts[s] + WIN], 0.0, fill
        )
    gsum[...] = jnp.zeros_like(gsum)

    def step(block, carry):
        arrive(buf, sems, block)
        weight = buf.at[block]
        gmix[...] = dot(branch[...], weight[:, width:]).astype(bf16)
        for h in range(heads):
            parts = []
            cols = [slice(c * inner + h * HD, c * inner + (h + 1) * HD) for c in range(3)]
            for s in range(2):
                rows = slice(starts[s], starts[s] + WIN)
                q, k, v = (qkv_all[block, rows, c] for c in cols)
                q = q * bf16(HD**-0.5)
                k_scaled = k * bf16(HD**-0.5)
                g = gmix[rows, h * HD : (h + 1) * HD]
                scores = dot(k, q, NT) + bias[s]
                top = jnp.maximum(jnp.max(scores, axis=0, keepdims=True), floor)
                weights = jnp.exp(scores - top)
                total = jnp.maximum(jnp.sum(weights, axis=0, keepdims=True), 1e-30)
                probs = weights * (1.0 / total)
                grad_probs = dot(v, g, NT)
                centre = jnp.sum(grad_probs * probs, axis=0, keepdims=True)
                grad_scores = (probs * (grad_probs - centre)).astype(bf16)
                parts.append(
                    (
                        dot(grad_scores, k_scaled, TN),
                        dot(grad_scores, q),
                        dot(probs.astype(bf16), g),
                    )
                )
            for c in range(3):
                gqkv[:, cols[c]] = join_windows(parts[0][c], parts[1][c], count).astype(bf16)
        gsum[...] += dot(gqkv[...], weight[:, :width], NT)
        return carry

    lax.fori_loop(0, buf.shape[0], step, 0)
    unit, scale = norm_parts(start[...].astype(f32))
    grad = grad_after[...] + norm_back(unit, scale, gsum[...], gain[...].astype(f32))
    idx = index[...]
    grad_tok[...] = jnp.where(idx >= 0, 0.0, grad).astype(bf16)
    lanes = lax.broadcasted_iota(jnp.int32, (count, grad_prm.shape[0]), 1)
    onehot = (idx == lanes).astype(f32).astype(bf16)
    high = grad.astype(bf16)
    rest_one = grad - high.astype(f32)
    middle = rest_one.astype(bf16)
    low = (rest_one - middle.astype(f32)).astype(bf16)
    grad_prm[...] = dot(onehot, high, TN) + dot(onehot, middle, TN) + dot(onehot, low, TN)


vmem = pl.BlockSpec(memory_space=pltpu.VMEM)
smem = pl.BlockSpec(memory_space=pltpu.SMEM)
hbm = pl.BlockSpec(memory_space=pl.ANY)


def shape(dims, kind):
    return jax.ShapeDtypeStruct(dims, kind)


def swap(value, axis, partner):
    size = lax.axis_size(axis)
    return lax.ppermute(value, axis, [(i, partner(i)) for i in range(size)])


def turn_z(value, by):
    return swap(value, "dp", lambda i: ((i // 2 + by) % 4) * 2 + i % 2)


def gather_blocks(shard):
    column = jnp.concatenate([shard] + [turn_z(shard, k) for k in (1, 2, 3)], 0)
    rows = column.shape[0]
    over_x = swap(column, "tp", lambda i: i ^ 2)
    over_y = swap(column, "dp", lambda i: i ^ 1)
    diag_x = swap(over_y[: rows // 2], "tp", lambda i: i ^ 2)
    diag_y = swap(over_x[rows // 2 :], "dp", lambda i: i ^ 1)
    mine = [column, over_y, over_x, diag_x, diag_y]
    other = [swap(piece, "tp", lambda i: i ^ 1) for piece in mine]
    return mine + other


def block_plan(rows):
    def piece(which, first, count, dy):
        return [(which, j * rows, rows, dy * 4 + first + j) for j in range(count)]

    plan = []
    for base in (0, 5):
        plan.append(piece(base, 0, 4, 0) + piece(base + 1, 0, 4, 1))
        plan.append(piece(base + 2, 0, 4, 0) + piece(base + 3, 0, 2, 1) + piece(base + 4, 2, 2, 1))
    return plan


def block_places(rows):
    here = lax.axis_index("dp")
    z, y = here // 2, here % 2
    k = jnp.arange(8, dtype=jnp.int32)
    return (((z - k % 4) % 4) * 2 + (y ^ (k // 4))) * rows


def on_device(
    tokens, prompt, qkv_weight, out_weight, up_weight, down_weight, gain_one, gain_two, segment_ids, pad_flags, cotangent
):
    dp, tp = lax.axis_size("dp"), lax.axis_size("tp")
    tok_dev, width = tokens.shape
    row_count, seq_len = segment_ids.shape
    count = tok_dev + HALO
    rows = qkv_weight.shape[0]
    inner = qkv_weight.shape[2]
    rank = lax.axis_index("tp")
    core = rank % 2
    row = rank // 2

    shard_a = jnp.concatenate([qkv_weight.reshape(rows, 3 * inner), out_weight.T], axis=1)
    shard_u = up_weight
    shard_d = down_weight.T
    if dp == 8:
        groups = [gather_blocks(s) for s in (shard_a, shard_u, shard_d)]
        plan = block_plan(rows)
        offs = block_places(rows)
    else:
        groups = []
        for s in (shard_a, shard_u, shard_d):
            whole = lax.all_gather(lax.all_gather(s, "dp", axis=0, tiled=True), "tp", axis=0, tiled=True)
            groups.append([whole])
        plan = [[(0, t * width, width, 0)] for t in range(tp)]
        offs = jnp.zeros((8,), jnp.int32)

    sent = (1 - core) * (tok_dev - HALO)
    both = jnp.concatenate(
        [
            lax.dynamic_slice_in_dim(tokens, sent, HALO, 0),
            lax.dynamic_slice_in_dim(cotangent, sent, HALO, 0),
        ],
        0,
    )
    both = swap(both, "tp", lambda i: i ^ 1)
    main, side = HALO * core, tok_dev * (1 - core)
    place = jnp.stack([main, side]).astype(jnp.int32)

    first = core * (seq_len - count)
    seg = lax.dynamic_slice(segment_ids, (row, first), (1, count))
    pad = lax.dynamic_slice(pad_flags, (row, first), (1, count))
    position = jnp.arange(count, dtype=jnp.int32)[None, :]
    live = pad == 0
    keys = [jnp.where(live & (seg == 2 * core + s), seg, -1) for s in range(2)]
    index = jnp.full((1, count), -1, jnp.int32)
    for s in range(2):
        begin = jnp.min(jnp.where(keys[s] >= 0, position, count))
        offset = position - begin
        index = jnp.where((keys[s] >= 0) & (offset >= 1) & (offset <= PROMPTS), offset - 1, index)
    column = lambda r: r.reshape(count, 1)
    index_col = column(index)

    gain_one, gain_two = gain_one[None, :], gain_two[None, :]
    start, normed, cot = pl.pallas_call(
        enter_kernel,
        name="enter",
        in_specs=[smem] + [vmem] * 7,
        out_specs=[vmem] * 3,
        out_shape=[shape((count, width), bf16)] * 3,
    )(place, tokens, both[:HALO], cotangent, both[HALO:], prompt, index_col, gain_one)

    blocks = len(plan)
    dma = pltpu.SemaphoreType.DMA
    after, normed_two, qkv_all = pl.pallas_call(
        functools.partial(attend_kernel, plan),
        name="attend",
        in_specs=[smem] + [vmem] * 6 + [hbm] * len(groups[0]),
        out_specs=[vmem] * 3,
        out_shape=[shape((count, width), f32), shape((count, width), bf16), shape((blocks, count, 3 * inner), bf16)],
        scratch_shapes=[
            pltpu.VMEM((blocks, width, width), bf16),
            pltpu.VMEM((2, WIN, WIN), f32),
            pltpu.VMEM((count, inner), bf16),
            dma((blocks,)),
        ],
    )(offs, normed, start, gain_two, column(seg), keys[0], keys[1], *groups[0])

    output, grad_after, branch = pl.pallas_call(
        functools.partial(mlp_kernel, plan),
        name="mlp",
        in_specs=[smem] + [vmem] * 4 + [hbm] * (len(groups[1]) + len(groups[2])),
        out_specs=[vmem] * 3,
        out_shape=[shape((count, width), bf16), shape((count, width), f32), shape((count, width), bf16)],
        scratch_shapes=[
            pltpu.VMEM((blocks, width, width), bf16),
            pltpu.VMEM((blocks, width, width), bf16),
            pltpu.VMEM((count, width), f32),
            pltpu.VMEM((count, width), f32),
            dma((2, blocks)),
        ],
    )(offs, normed_two, cot, after, gain_two, *groups[1], *groups[2])

    grad_tok, grad_prm = pl.pallas_call(
        functools.partial(back_kernel, plan),
        name="back",
        in_specs=[smem] + [vmem] * 9 + [hbm] * len(groups[0]),
        out_specs=[vmem] * 2,
        out_shape=[shape((count, width), bf16), shape((64, width), f32)],
        scratch_shapes=[
            pltpu.VMEM((blocks, width, width), bf16),
            pltpu.VMEM((2, WIN, WIN), f32),
            pltpu.VMEM((count, inner), bf16),
            pltpu.VMEM((count, 3 * inner), bf16),
            pltpu.VMEM((count, width), f32),
            dma((blocks,)),
        ],
    )(offs, branch, grad_after, start, qkv_all, gain_one, seg, column(keys[0]), column(keys[1]), index_col, *groups[0])

    seam = core * 0 + sent
    mine = lax.dynamic_slice_in_dim(column(seg), main + seam, HALO, 0) // 2 == core

    def settle(window):
        theirs = swap(lax.dynamic_slice_in_dim(window, side, HALO, 0), "tp", lambda i: i ^ 1)
        own = lax.dynamic_slice_in_dim(window, main, tok_dev, 0)
        kept = lax.dynamic_slice_in_dim(own, seam, HALO, 0)
        return lax.dynamic_update_slice_in_dim(own, jnp.where(mine, kept, theirs), seam, 0)

    output = settle(output)
    grad_tok = settle(grad_tok)
    if dp == 8:
        prm = grad_prm + swap(grad_prm, "tp", lambda i: i ^ 1)
        prm = prm + swap(prm, "tp", lambda i: i ^ 2)
        prm = prm + swap(prm, "dp", lambda i: i ^ 1)
        prm = prm + turn_z(prm, 1) + turn_z(prm, 2) + turn_z(prm, 3)
    else:
        prm = lax.psum(grad_prm, ("dp", "tp"))
    grad_prm = (prm[:PROMPTS] / (row_count * dp)).astype(bf16)
    return (output, grad_tok, grad_prm)


def solution(mesh):
    return jax.shard_map(
        on_device,
        mesh=mesh,
        in_specs=(
            P(("dp", "tp"), None),
            P(),
            P("dp", None, "tp"),
            P("tp", "dp"),
            P("dp", "tp"),
            P("tp", "dp"),
            P(),
            P(),
            P("dp", None),
            P("dp", None),
            P(("dp", "tp"), None),
        ),
        out_specs=(P(("dp", "tp"), None), P(("dp", "tp"), None), P()),
        check_vma=False,
    )
```

```python
import functools

import jax
import jax.numpy as jnp
from jax import lax
from jax.experimental import pallas as pl
from jax.experimental.pallas import tpu as pltpu
from jax.sharding import PartitionSpec as P

HD = 64
PROMPTS = 50
HALO = 32
WIN = 304
KEYS = 256
SLACK = 8
NT = (((1,), (1,)), ((), ()))
NN = (((1,), (0,)), ((), ()))
TN = (((0,), (0,)), ((), ()))
eps = 1e-6
fill = -1e30
floor = -1e29
bf16 = jnp.bfloat16
f32 = jnp.float32


def dot(a, b, dims=NN):
    return lax.dot_general(a, b, dims, preferred_element_type=f32)


def norm_parts(values):
    centred = values - jnp.mean(values, axis=-1, keepdims=True)
    scale = lax.rsqrt(jnp.mean(centred * centred, axis=-1, keepdims=True) + eps)
    return centred * scale, scale


def norm_back(unit, scale, grad, gain):
    u = grad * gain
    return scale * (
        u - jnp.mean(u, axis=-1, keepdims=True) - unit * jnp.mean(u * unit, axis=-1, keepdims=True)
    )


def window_starts(count):
    return (0, count - WIN)


def join_windows(first, second, count):
    low = count - WIN
    return jnp.concatenate([first[:low], first[low:] + second[: WIN - low], second[WIN - low :]], 0)


def fetch(plan, table, refs, buf, sems):
    for which, source, rows, slot, block, lane in plan:
        lanes = refs[which].shape[1]
        pltpu.make_async_copy(
            refs[which].at[pl.ds(source, rows)],
            buf.at[block, pl.ds(pl.multiple_of(table[slot], 16), rows), pl.ds(lane, lanes)],
            sems.at[block],
        ).start()


def arrive(buf, sems, block):
    pltpu.make_async_copy(buf.at[block], buf.at[block], sems.at[block]).wait()


def shifted_in(wide, place, s):
    low = pl.multiple_of(place[2 + s], SLACK)
    value = wide[pl.ds(low, KEYS + SLACK), :]
    return pltpu.roll(value, place[6 + s], 0)[:KEYS]


def enter_kernel(place, own, own_halo, cot, cot_halo, prompt, index, gain, start, normed, cot_out):
    main = pl.multiple_of(place[0], HALO)
    side = pl.multiple_of(place[1], HALO)
    rows = own.shape[0]
    start[pl.ds(main, rows), :] = own[...]
    start[pl.ds(side, HALO), :] = own_halo[...]
    cot_out[pl.ds(main, rows), :] = cot[...]
    cot_out[pl.ds(side, HALO), :] = cot_halo[...]
    idx = index[...]
    lanes = lax.broadcasted_iota(jnp.int32, (idx.shape[0], PROMPTS), 1)
    onehot = (idx == lanes).astype(f32).astype(bf16)
    picked = dot(onehot, prompt[...])
    value = jnp.where(idx >= 0, picked, start[...].astype(f32))
    start[...] = value.astype(bf16)
    unit, _ = norm_parts(value)
    normed[...] = (unit * gain[...].astype(f32)).astype(bf16)


def attend_kernel(plan, place, table, normed, start, gain, qseg, krow_a, krow_b, *rest):
    n = len(rest) - 9
    refs, (after, normed_two, q_out, kv_out, buf, bias, mix, wide, sems) = rest[:n], rest[n:]
    count = normed.shape[0]
    inner = q_out.shape[2]
    heads = inner // HD
    fetch(plan, table, refs, buf, sems)
    starts = window_starts(count)
    for s, krow in enumerate((krow_a, krow_b)):
        bias[s] = jnp.where(qseg[starts[s] : starts[s] + WIN, :] == krow[...], 0.0, fill)
    after[...] = start[...].astype(f32)
    wide[count:] = jnp.zeros_like(wide[count:])

    def step(block, carry):
        arrive(buf, sems, block)
        weight = buf.at[block]
        both = dot(normed[...], weight[:, : 3 * inner])
        q_all = both[:, :inner].astype(bf16) * bf16(HD**-0.5)
        q_out[block] = q_all
        wide[:count] = both[:, inner:]
        pairs = [shifted_in(wide, place, s).astype(bf16) for s in range(2)]
        for s in range(2):
            kv_out[block, s] = pairs[s]
        for h in range(heads):
            parts = []
            for s in range(2):
                q = q_all[starts[s] : starts[s] + WIN, h * HD : (h + 1) * HD]
                k = pairs[s][:, h * HD : (h + 1) * HD]
                v = pairs[s][:, inner + h * HD : inner + (h + 1) * HD]
                scores = dot(q, k, NT) + bias[s]
                top = jnp.maximum(jnp.max(scores, axis=-1, keepdims=True), floor)
                weights = jnp.exp(scores - top)
                total = jnp.maximum(jnp.sum(weights, axis=-1, keepdims=True), 1e-30)
                probs = (weights * (1.0 / total)).astype(bf16)
                parts.append(dot(probs, v))
            mix[:, h * HD : (h + 1) * HD] = join_windows(parts[0], parts[1], count).astype(bf16)
        after[...] += dot(mix[...], weight[:, 3 * inner :], NT)
        return carry

    lax.fori_loop(0, buf.shape[0], step, 0)
    unit, _ = norm_parts(after[...])
    normed_two[...] = (unit * gain[...].astype(f32)).astype(bf16)


def mlp_kernel(plans, first, last, table, normed_two, cot, total_in, gsum_in, after, gain, *rest):
    n = len(rest) - (8 if last else 5)
    refs, rest = rest[:n], rest[n:]
    if last:
        output, grad_after, branch, total, gsum, up, down, sems = rest
    else:
        total, gsum, up, down, sems = rest
    fetch(plans[0], table, refs, up, sems.at[0])
    fetch(plans[1], table, refs, down, sems.at[1])
    arrive(up, sems.at[0], 0)
    pre = dot(normed_two[...], up[0])
    cdf = 0.5 + 0.5 * lax.erf(pre * (0.5**0.5))
    slope = cdf + pre * (jnp.exp(-0.5 * pre * pre) * 0.3989422804014327)
    act = (pre * cdf).astype(bf16)
    arrive(down, sems.at[1], 0)
    back = dot(cot[...], down[0])
    grad_pre = (back * slope).astype(bf16)
    total[...] = total_in[...] + dot(act, down[0], NT)
    gain_sum = dot(grad_pre, up[0], NT)
    gsum[...] = gain_sum if first else gsum_in[...] + gain_sum
    if last:
        output[...] = total[...].astype(bf16)
        unit, scale = norm_parts(after[...])
        grad = cot[...].astype(f32) + norm_back(unit, scale, gsum[...], gain[...].astype(f32))
        grad_after[...] = grad
        branch[...] = grad.astype(bf16)


def back_kernel(plan, place, table, branch, grad_after, start, q_all, kv_all, gain, qrow, kcol_a, kcol_b, index, *rest):
    n = len(rest) - 10
    refs, (grad_tok, grad_prm, buf, bias, gmix, gq, gkv, gqkv, gsum, sems) = rest[:n], rest[n:]
    count = branch.shape[0]
    inner = q_all.shape[2]
    heads = inner // HD
    fetch(plan, table, refs, buf, sems)
    starts = window_starts(count)
    for s, kcol in enumerate((kcol_a, kcol_b)):
        bias[s] = jnp.where(kcol[...] == qrow[...][:, starts[s] : starts[s] + WIN], 0.0, fill)
    gsum[...] = jnp.zeros_like(gsum)
    gkv[...] = jnp.zeros_like(gkv)

    def step(block, carry):
        arrive(buf, sems, block)
        weight = buf.at[block]
        gmix[...] = dot(branch[...], weight[:, 3 * inner :]).astype(bf16)
        for h in range(heads):
            cols = slice(h * HD, (h + 1) * HD)
            late = slice(inner + h * HD, inner + (h + 1) * HD)
            parts = []
            for s in range(2):
                rows = slice(starts[s], starts[s] + WIN)
                q = q_all[block, rows, cols]
                k = kv_all[block, s, :, cols]
                v = kv_all[block, s, :, late]
                g = gmix[rows, cols]
                scores = dot(k, q, NT) + bias[s]
                top = jnp.maximum(jnp.max(scores, axis=0, keepdims=True), floor)
                weights = jnp.exp(scores - top)
                total = jnp.maximum(jnp.sum(weights, axis=0, keepdims=True), 1e-30)
                probs = weights * (1.0 / total)
                grad_probs = dot(v, g, NT)
                centre = jnp.sum(grad_probs * probs, axis=0, keepdims=True)
                grad_scores = (probs * (grad_probs - centre)).astype(bf16)
                parts.append(dot(grad_scores, k * bf16(HD**-0.5), TN))
                gkv[s, :KEYS, cols] = dot(grad_scores, q)
                gkv[s, :KEYS, late] = dot(probs.astype(bf16), g)
            gqkv[:, cols] = join_windows(parts[0], parts[1], count).astype(bf16)
        gq[...] = jnp.zeros_like(gq)
        for s in range(2):
            low = pl.multiple_of(place[2 + s], SLACK)
            gq[pl.ds(low, KEYS + SLACK), :] += pltpu.roll(gkv[s], place[4 + s], 0)
        gqkv[:, inner:] = gq[:count].astype(bf16)
        gsum[...] += dot(gqkv[...], weight[:, : 3 * inner], NT)
        return carry

    lax.fori_loop(0, buf.shape[0], step, 0)
    unit, scale = norm_parts(start[...].astype(f32))
    grad = grad_after[...] + norm_back(unit, scale, gsum[...], gain[...].astype(f32))
    idx = index[...]
    grad_tok[...] = jnp.where(idx >= 0, 0.0, grad).astype(bf16)
    lanes = lax.broadcasted_iota(jnp.int32, (count, grad_prm.shape[0]), 1)
    onehot = (idx == lanes).astype(f32).astype(bf16)
    high = grad.astype(bf16)
    rest_one = grad - high.astype(f32)
    middle = rest_one.astype(bf16)
    low = (rest_one - middle.astype(f32)).astype(bf16)
    grad_prm[...] = dot(onehot, high, TN) + dot(onehot, middle, TN) + dot(onehot, low, TN)


vmem = pl.BlockSpec(memory_space=pltpu.VMEM)
smem = pl.BlockSpec(memory_space=pltpu.SMEM)
hbm = pl.BlockSpec(memory_space=pl.ANY)


def outside(arrays):
    return [pltpu.with_memory_space_constraint(a, pltpu.HBM) for a in arrays]


def shape(dims, kind):
    return jax.ShapeDtypeStruct(dims, kind)


def cost(flops, moved, exps=0):
    return pl.CostEstimate(flops=int(flops), bytes_accessed=int(moved), transcendentals=int(exps))


def move(value, target):
    pairs = []
    for i in range(32):
        z, y, x, c = target(i // 8, i // 4 % 2, i // 2 % 2, i % 2)
        pairs.append((i, ((z * 2 + y) * 2 + x) * 2 + c))
    return lax.ppermute(value, ("dp", "tp"), pairs)


def by_z(value, bits):
    return move(value, lambda z, y, x, c: (z ^ bits, y, x, c))


def by_x(value):
    return move(value, lambda z, y, x, c: (z, y, x ^ 1, c))


def by_y(value):
    return move(value, lambda z, y, x, c: (z, y ^ 1, x, c))


def split_xy(value):
    return move(value, lambda z, y, x, c: (z, y, x ^ 1, c) if c == 0 else (z, y ^ 1, x, c))


def split_yx(value):
    return move(value, lambda z, y, x, c: (z, y ^ 1, x, c) if c == 0 else (z, y, x ^ 1, c))


def across(value):
    axis = "tp"
    size = lax.axis_size(axis)
    return lax.ppermute(value, axis, [(i, i ^ 1) for i in range(size)])


def stack(pieces):
    return jnp.concatenate(pieces, 0)


def tie(value, *deps):
    return lax.optimization_barrier((value,) + deps)[0]


def by_core(even, odd):
    return jnp.where(lax.axis_index("tp") % 2 == 0, even, odd)


def places(rows):
    here = lax.axis_index("dp")
    slots = jnp.arange(8, dtype=jnp.int32)
    return (((here // 2) ^ (slots % 4)) * 2 + ((here % 2) ^ (slots // 4))) * rows


def column_plan(which, dy, block, lane, rows, sub=0, subs=1):
    return [(which, (j * subs + sub) * rows, rows, dy * 4 + j, block, lane) for j in range(4)]


def quad_plan(which, z, rows, dx, block, lane):
    return [(which, (dx + 2 * dy) * rows, rows, dy * 4 + z, block, lane) for dy in range(2)]


def on_device(
    tokens, prompt, qkv_weight, out_weight, up_weight, down_weight, gain_one, gain_two, segment_ids, pad_flags, cotangent
):
    dp, tp = lax.axis_size("dp"), lax.axis_size("tp")
    tok_dev, width = tokens.shape
    row_count, seq_len = segment_ids.shape
    count = tok_dev + HALO
    rows = qkv_weight.shape[0]
    inner = qkv_weight.shape[2]
    hidden = up_weight.shape[1]
    rank = lax.axis_index("tp")
    core = rank % 2
    row = rank // 2

    shard_a = jnp.concatenate([qkv_weight.reshape(rows, 3 * inner), out_weight.T], axis=1)
    shard_d = down_weight.T
    half = hidden // 2
    up_one, up_two = up_weight[:, :half], up_weight[:, half:]
    down_one, down_two = shard_d[:, :half], shard_d[:, half:]

    sent = (1 - core) * (tok_dev - HALO)
    both = stack(
        [
            lax.dynamic_slice_in_dim(tokens, sent, HALO, 0),
            lax.dynamic_slice_in_dim(cotangent, sent, HALO, 0),
        ]
    )
    both = across(both)
    main, side = HALO * core, tok_dev * (1 - core)

    first = core * (seq_len - count)
    seg = lax.dynamic_slice(segment_ids, (row, first), (1, count))
    pad = lax.dynamic_slice(pad_flags, (row, first), (1, count))
    position = jnp.arange(count, dtype=jnp.int32)[None, :]
    live = pad == 0
    index = jnp.full((1, count), -1, jnp.int32)
    begins, keys = [], []
    for s in range(2):
        own = live & (seg == 2 * core + s)
        begin = jnp.min(jnp.where(own, position, count))
        offset = position - begin
        index = jnp.where(own & (offset >= 1) & (offset <= PROMPTS), offset - 1, index)
        begins.append(jnp.minimum(begin, count - KEYS))
        keys.append(lax.dynamic_slice(jnp.where(own, seg, -1), (0, begins[s]), (1, KEYS)))
    column = lambda r: r.reshape(r.shape[1], 1)
    index_col = column(index)
    lows = [b // SLACK * SLACK for b in begins]
    shifts = [b - a for a, b in zip(lows, begins)]
    back_shifts = [(KEYS + SLACK - b) % (KEYS + SLACK) for b in shifts]
    place = jnp.stack([main, side] + lows + shifts + back_shifts).astype(jnp.int32)

    gain_one, gain_two = gain_one[None, :], gain_two[None, :]
    limit = lambda mib: pltpu.CompilerParams(vmem_limit_bytes=mib << 20)
    act = count * width
    mac = 2 * act * width
    start, normed, cot = pl.pallas_call(
        enter_kernel,
        name="enter",
        in_specs=[smem] + [vmem] * 7,
        out_specs=[vmem] * 3,
        out_shape=[pltpu.HBM((count, width), bf16)] * 3,
        cost_estimate=cost(2 * act * 64, 10 * act),
        compiler_params=limit(12),
    )(place, tokens, both[:HALO], cotangent, both[HALO:], prompt, index_col, gain_one)

    blocks = tp
    heads = width // HD
    dma = pltpu.SemaphoreType.DMA
    pair_flops = 2 * 2 * WIN * KEYS * HD * heads

    def attend(plan, arrays):
        return pl.pallas_call(
            functools.partial(attend_kernel, plan),
            name="attend",
            in_specs=[smem] * 2 + [vmem] * 6 + [hbm] * len(arrays),
            out_specs=[vmem] * 4,
            out_shape=[
                shape((count, width), f32),
                shape((count, width), bf16),
                pltpu.HBM((blocks, count, inner), bf16),
                pltpu.HBM((blocks, 2, KEYS, 2 * inner), bf16),
            ],
            scratch_shapes=[
                pltpu.VMEM((blocks, width, width), bf16),
                pltpu.VMEM((2, WIN, KEYS), f32),
                pltpu.VMEM((count, inner), bf16),
                pltpu.VMEM((count + SLACK, 2 * inner), f32),
                dma((blocks,)),
            ],
            cost_estimate=cost(4 * mac + 2 * pair_flops, 8 * width * width + 16 * act, 2 * WIN * KEYS * heads),
            compiler_params=limit(24),
        )(place, table, normed, start, gain_two, column(seg), *keys, *outside(arrays))

    def mlp(plans, arrays, total, gsum, first=False, last=False):
        outs = [shape((count, width), f32)] * 2
        if last:
            outs = [shape((count, width), bf16), shape((count, width), f32), shape((count, width), bf16)]
        sums = [pltpu.VMEM((count, width), f32)] * 2 if last else []
        return pl.pallas_call(
            functools.partial(mlp_kernel, plans, first, last),
            name="mlp_last" if last else "mlp",
            in_specs=[smem] + [vmem] * 6 + [hbm] * len(arrays),
            out_specs=[vmem] * len(outs),
            out_shape=outs,
            scratch_shapes=sums + [pltpu.VMEM((1, width, width), bf16)] * 2 + [dma((2, 1))],
            cost_estimate=cost(4 * mac, 4 * width * width + 20 * act, 2 * act),
            compiler_params=limit(24),
        )(table, normed_two, cot, total, gsum, after, gain_two, *outside(arrays))

    if dp == 8:
        table = places(rows)
        a_one, a_two = by_z(shard_a, 1), by_z(shard_a, 2)
        d_x, d_y = by_x(down_two), by_y(down_two)
        a_three = by_z(a_two, 1)
        a_col = tie(stack([shard_a, a_one, a_two, a_three]), d_x, d_y)
        a_x, a_y = by_x(a_col), by_y(a_col)
        m_own = tie(stack([up_one, down_one, up_two]), a_col)
        m_one, m_two = by_z(m_own, 1), by_z(m_own, 2)
        a_diag = split_yx(tie(by_core(a_x, a_y), m_one, m_two, normed))
        m_three = by_z(tie(m_two, a_col), 1)
        d_diag = split_yx(tie(by_core(d_x, d_y), a_col))
        a_pairs = [(v, across(v)) for v in (a_col, a_x, a_y, a_diag)]
        arrays_a, plan_a = [], []
        for which, pair in enumerate(a_pairs):
            for dc, array in enumerate(pair):
                plan_a += column_plan(len(arrays_a), which // 2, (which % 2) * 2 + dc, 0, rows)
                arrays_a.append(array)
        cols = [m_own, m_one, m_two, m_three]
        m_col = tie(stack([c[: 2 * rows] for c in cols]), a_diag)
        u_col = tie(stack([c[2 * rows :] for c in cols]), a_diag)
        d_quad = tie(stack([down_two, d_x, d_y, d_diag]), a_diag)
        m_x, m_y = by_x(m_col), by_y(m_col)
        u_x, u_y = by_x(u_col), by_y(u_col)
        d_one, d_two = by_z(d_quad, 1), by_z(d_quad, 2)
        arrays_a[0] = tie(arrays_a[0], m_col, u_col, d_quad)
        after, normed_two, q_all, kv_all = attend(plan_a, arrays_a)
        m_x, m_y, u_x, u_y, d_two = lax.optimization_barrier((m_x, m_y, u_x, u_y, d_two, normed_two))[:5]
        m_diag = split_yx(by_core(m_x, m_y))
        u_diag = split_yx(by_core(u_x, u_y))
        d_three = by_z(d_two, 1)
        d_parts = []
        for part in (d_quad, d_one, d_two, d_three):
            d_parts += [part, across(part)]

        def m_call(dx, near, far, total, gsum, first):
            arrays = [near, across(near), far, across(far)]
            plans = [
                [e for k in range(4) for e in column_plan(k, k // 2, 0, (k % 2) * half, rows, sub, 2)] for sub in range(2)
            ]
            return mlp(plans, arrays, total, gsum, first)

        def u_call(dx, near, far, total, gsum, last):
            arrays = [near, across(near), far, across(far)] + d_parts
            plans = [
                [e for k in range(4) for e in column_plan(k, k // 2, 0, (k % 2) * half, rows)],
                [e for k in range(8) for e in quad_plan(4 + k, k // 2, rows, dx, 0, (k % 2) * half)],
            ]
            return mlp(plans, arrays, total, gsum, False, last)

        total, gsum = m_call(0, m_col, m_y, after, after, True)
        total, gsum = u_call(0, u_col, u_y, total, gsum, False)
        total, gsum = m_call(1, m_x, m_diag, total, gsum, False)
        output, grad_after, branch = u_call(1, u_x, u_diag, total, gsum, True)
    else:
        table = jnp.zeros((8,), jnp.int32)

        def whole(shard):
            return lax.all_gather(lax.all_gather(shard, "dp", axis=0, tiled=True), "tp", axis=0, tiled=True)

        arrays_a, plan_a = [whole(shard_a)], [(0, t * width, width, 0, t, 0) for t in range(tp)]
        after, normed_two, q_all, kv_all = attend(plan_a, arrays_a)
        pairs = [(whole(up_one), whole(down_one)), (whole(up_two), whole(down_two))]
        total, gsum = after, after
        for k in range(4):
            plans = [[(i, (k % 2 * 2 + dc) * width, width, 0, 0, dc * half) for dc in range(2)] for i in range(2)]
            total, gsum, *extra = mlp(plans, list(pairs[k // 2]), total, gsum, k == 0, k == 3)
        output, grad_after, branch = total, gsum, extra[0]

    grad_tok, grad_prm = pl.pallas_call(
        functools.partial(back_kernel, plan_a),
        name="back",
        in_specs=[smem] * 2 + [vmem] * 10 + [hbm] * len(arrays_a),
        out_specs=[vmem] * 2,
        out_shape=[shape((count, width), bf16), shape((64, width), f32)],
        scratch_shapes=[
            pltpu.VMEM((blocks, width, width), bf16),
            pltpu.VMEM((2, KEYS, WIN), f32),
            pltpu.VMEM((count, inner), bf16),
            pltpu.VMEM((count + SLACK, 2 * inner), f32),
            pltpu.VMEM((2, KEYS + SLACK, 2 * inner), f32),
            pltpu.VMEM((count, 3 * inner), bf16),
            pltpu.VMEM((count, width), f32),
            dma((blocks,)),
        ],
        cost_estimate=cost(4 * mac + 5 * pair_flops, 8 * width * width + 16 * act, 2 * WIN * KEYS * heads),
        compiler_params=limit(32),
    )(
        place, table, branch, grad_after, start, q_all, kv_all, gain_one, seg, column(keys[0]), column(keys[1]), index_col,
        *outside(arrays_a),
    )

    mine = lax.dynamic_slice_in_dim(column(seg), main + sent, HALO, 0) // 2 == core

    def settle(window):
        theirs = across(lax.dynamic_slice_in_dim(window, side, HALO, 0))
        own = lax.dynamic_slice_in_dim(window, main, tok_dev, 0)
        kept = lax.dynamic_slice_in_dim(own, sent, HALO, 0)
        return lax.dynamic_update_slice_in_dim(own, jnp.where(mine, kept, theirs), sent, 0)

    prm = grad_prm[:PROMPTS]
    if dp == 8:
        for step in (across, by_x, by_y, lambda v: by_z(v, 1), lambda v: by_z(v, 2)):
            sent_prm = prm.astype(bf16)
            prm = sent_prm.astype(f32) + step(sent_prm).astype(f32)
    else:
        prm = lax.psum(prm, ("dp", "tp"))
    grad_prm = (prm / (row_count * dp)).astype(bf16)
    return (settle(output), settle(grad_tok), grad_prm)


def solution(mesh):
    return jax.shard_map(
        on_device,
        mesh=mesh,
        in_specs=(
            P(("dp", "tp"), None),
            P(),
            P("dp", None, "tp"),
            P("tp", "dp"),
            P("dp", "tp"),
            P("tp", "dp"),
            P(),
            P(),
            P("dp", None),
            P("dp", None),
            P(("dp", "tp"), None),
        ),
        out_specs=(P(("dp", "tp"), None), P(("dp", "tp"), None), P()),
        check_vma=False,
    )
```

```python
import functools

import jax
import jax.numpy as jnp
from jax import lax
from jax.experimental import pallas as pl
from jax.experimental.pallas import tpu as pltpu
from jax.sharding import PartitionSpec as P

HD = 64
PROMPTS = 50
HALO = 32
WIN = 304
KEYS = 256
SLACK = 8
NT = (((1,), (1,)), ((), ()))
NN = (((1,), (0,)), ((), ()))
TN = (((0,), (0,)), ((), ()))
eps = 1e-6
fill = -1e30
floor = -1e29
bf16 = jnp.bfloat16
f32 = jnp.float32


def dot(a, b, dims=NN):
    return lax.dot_general(a, b, dims, preferred_element_type=f32)


def norm_parts(values):
    centred = values - jnp.mean(values, axis=-1, keepdims=True)
    scale = lax.rsqrt(jnp.mean(centred * centred, axis=-1, keepdims=True) + eps)
    return centred * scale, scale


def norm_back(unit, scale, grad, gain):
    u = grad * gain
    return scale * (
        u - jnp.mean(u, axis=-1, keepdims=True) - unit * jnp.mean(u * unit, axis=-1, keepdims=True)
    )


def window_starts(count):
    return (0, count - WIN)


def join_windows(first, second, count):
    low = count - WIN
    return jnp.concatenate([first[:low], first[low:] + second[: WIN - low], second[WIN - low :]], 0)


def fetch(plan, table, refs, buf, sems):
    for which, source, rows, slot, block, lane in plan:
        lanes = refs[which].shape[1]
        pltpu.make_async_copy(
            refs[which].at[pl.ds(source, rows)],
            buf.at[block, pl.ds(pl.multiple_of(table[slot], 16), rows), pl.ds(lane, lanes)],
            sems.at[block],
        ).start()


def arrive(buf, sems, block):
    pltpu.make_async_copy(buf.at[block], buf.at[block], sems.at[block]).wait()


def shifted_in(wide, place, s):
    low = pl.multiple_of(place[2 + s], SLACK)
    value = wide[pl.ds(low, KEYS + SLACK), :]
    return pltpu.roll(value, place[6 + s], 0)[:KEYS]


def enter_kernel(place, own, own_halo, cot, cot_halo, prompt, index, gain, start, normed, cot_out):
    main = pl.multiple_of(place[0], HALO)
    side = pl.multiple_of(place[1], HALO)
    rows = own.shape[0]
    start[pl.ds(main, rows), :] = own[...]
    start[pl.ds(side, HALO), :] = own_halo[...]
    cot_out[pl.ds(main, rows), :] = cot[...]
    cot_out[pl.ds(side, HALO), :] = cot_halo[...]
    idx = index[...]
    lanes = lax.broadcasted_iota(jnp.int32, (idx.shape[0], PROMPTS), 1)
    onehot = (idx == lanes).astype(f32).astype(bf16)
    picked = dot(onehot, prompt[...])
    value = jnp.where(idx >= 0, picked, start[...].astype(f32))
    start[...] = value.astype(bf16)
    unit, _ = norm_parts(value)
    normed[...] = (unit * gain[...].astype(f32)).astype(bf16)


def attend_kernel(plan, place, table, normed, start, gain, qseg, krow_a, krow_b, *rest):
    n = len(rest) - 12
    refs, (after, normed_two, q_out, kv_out, buf, bias, mix, wide, normed_in, start_in, sems, own_sems) = rest[:n], rest[n:]
    count = normed.shape[0]
    inner = q_out.shape[2]
    heads = inner // HD
    own = [
        pltpu.make_async_copy(normed, normed_in, own_sems.at[0]),
        pltpu.make_async_copy(start, start_in, own_sems.at[1]),
    ]
    for copy in own:
        copy.start()
    fetch(plan, table, refs, buf, sems)
    starts = window_starts(count)
    for s, krow in enumerate((krow_a, krow_b)):
        bias[s] = jnp.where(qseg[starts[s] : starts[s] + WIN, :] == krow[...], 0.0, fill)
    wide[count:] = jnp.zeros_like(wide[count:])
    for copy in own:
        copy.wait()
    after[...] = start_in[...].astype(f32)

    def step(block, carry):
        arrive(buf, sems, block)
        weight = buf.at[block]
        both = dot(normed_in[...], weight[:, : 3 * inner])
        q_all = both[:, :inner].astype(bf16) * bf16(HD**-0.5)
        q_out[block] = q_all
        wide[:count] = both[:, inner:]
        pairs = [shifted_in(wide, place, s).astype(bf16) for s in range(2)]
        for s in range(2):
            kv_out[block, s] = pairs[s]
        for h in range(heads):
            parts = []
            for s in range(2):
                q = q_all[starts[s] : starts[s] + WIN, h * HD : (h + 1) * HD]
                k = pairs[s][:, h * HD : (h + 1) * HD]
                v = pairs[s][:, inner + h * HD : inner + (h + 1) * HD]
                scores = dot(q, k, NT) + bias[s]
                top = jnp.maximum(jnp.max(scores, axis=-1, keepdims=True), floor)
                weights = jnp.exp(scores - top)
                total = jnp.maximum(jnp.sum(weights, axis=-1, keepdims=True), 1e-30)
                probs = (weights * (1.0 / total)).astype(bf16)
                parts.append(dot(probs, v))
            mix[:, h * HD : (h + 1) * HD] = join_windows(parts[0], parts[1], count).astype(bf16)
        after[...] += dot(mix[...], weight[:, 3 * inner :], NT)
        return carry

    lax.fori_loop(0, buf.shape[0], step, 0)
    unit, _ = norm_parts(after[...])
    normed_two[...] = (unit * gain[...].astype(f32)).astype(bf16)


def mlp_kernel(plans, last, table, normed_two, cot, total_in, gsum_in, after, gain, *rest):
    n = len(rest) - (8 if last else 5)
    refs, rest = rest[:n], rest[n:]
    if last:
        output, grad_after, branch, total, gsum, up, down, sems = rest
    else:
        total, gsum, up, down, sems = rest
    fetch(plans[0], table, refs, up, sems.at[0])
    fetch(plans[1], table, refs, down, sems.at[1])
    if last:
        total[...] = total_in[...]
        gsum[...] = gsum_in[...]

    def step(block, carry):
        arrive(up, sems.at[0], block)
        pre = dot(normed_two[...], up[block])
        cdf = 0.5 + 0.5 * lax.erf(pre * (0.5**0.5))
        slope = cdf + pre * (jnp.exp(-0.5 * pre * pre) * 0.3989422804014327)
        act = (pre * cdf).astype(bf16)
        arrive(down, sems.at[1], block)
        back = dot(cot[...], down[block])
        grad_pre = (back * slope).astype(bf16)
        before, grad_before = (total, gsum[...]) if last else (total_in, 0.0)
        total[...] = before[...] + dot(act, down[block], NT)
        gsum[...] = grad_before + dot(grad_pre, up[block], NT)
        return carry

    if last:
        lax.fori_loop(0, up.shape[0], step, 0)
    else:
        step(0, 0)
    if last:
        output[...] = total[...].astype(bf16)
        unit, scale = norm_parts(after[...])
        grad = cot[...].astype(f32) + norm_back(unit, scale, gsum[...], gain[...].astype(f32))
        grad_after[...] = grad
        branch[...] = grad.astype(bf16)


def back_kernel(plan, place, table, branch, grad_after, start, q_all, kv_all, gain, qrow, kcol_a, kcol_b, index, *rest):
    n = len(rest) - 10
    refs, (grad_tok, grad_prm, buf, bias, gmix, gq, gkv, gqkv, gsum, sems) = rest[:n], rest[n:]
    count = branch.shape[0]
    inner = q_all.shape[2]
    heads = inner // HD
    fetch(plan, table, refs, buf, sems)
    starts = window_starts(count)
    for s, kcol in enumerate((kcol_a, kcol_b)):
        bias[s] = jnp.where(kcol[...] == qrow[...][:, starts[s] : starts[s] + WIN], 0.0, fill)
    gsum[...] = jnp.zeros_like(gsum)
    gkv[...] = jnp.zeros_like(gkv)

    def step(block, carry):
        arrive(buf, sems, block)
        weight = buf.at[block]
        gmix[...] = dot(branch[...], weight[:, 3 * inner :]).astype(bf16)
        for h in range(heads):
            cols = slice(h * HD, (h + 1) * HD)
            late = slice(inner + h * HD, inner + (h + 1) * HD)
            parts = []
            for s in range(2):
                rows = slice(starts[s], starts[s] + WIN)
                q = q_all[block, rows, cols]
                k = kv_all[block, s, :, cols]
                v = kv_all[block, s, :, late]
                g = gmix[rows, cols]
                scores = dot(k, q, NT) + bias[s]
                top = jnp.maximum(jnp.max(scores, axis=0, keepdims=True), floor)
                weights = jnp.exp(scores - top)
                total = jnp.maximum(jnp.sum(weights, axis=0, keepdims=True), 1e-30)
                probs = weights * (1.0 / total)
                grad_probs = dot(v, g, NT)
                centre = jnp.sum(grad_probs * probs, axis=0, keepdims=True)
                grad_scores = (probs * (grad_probs - centre)).astype(bf16)
                parts.append(dot(grad_scores, k * bf16(HD**-0.5), TN))
                gkv[s, :KEYS, cols] = dot(grad_scores, q)
                gkv[s, :KEYS, late] = dot(probs.astype(bf16), g)
            gqkv[:, cols] = join_windows(parts[0], parts[1], count).astype(bf16)
        gq[...] = jnp.zeros_like(gq)
        for s in range(2):
            low = pl.multiple_of(place[2 + s], SLACK)
            gq[pl.ds(low, KEYS + SLACK), :] += pltpu.roll(gkv[s], place[4 + s], 0)
        gqkv[:, inner:] = gq[:count].astype(bf16)
        gsum[...] += dot(gqkv[...], weight[:, : 3 * inner], NT)
        return carry

    lax.fori_loop(0, buf.shape[0], step, 0)
    unit, scale = norm_parts(start[...].astype(f32))
    grad = grad_after[...] + norm_back(unit, scale, gsum[...], gain[...].astype(f32))
    idx = index[...]
    grad_tok[...] = jnp.where(idx >= 0, 0.0, grad).astype(bf16)
    lanes = lax.broadcasted_iota(jnp.int32, (count, grad_prm.shape[0]), 1)
    onehot = (idx == lanes).astype(f32).astype(bf16)
    high = grad.astype(bf16)
    rest_one = grad - high.astype(f32)
    middle = rest_one.astype(bf16)
    low = (rest_one - middle.astype(f32)).astype(bf16)
    grad_prm[...] = dot(onehot, high, TN) + dot(onehot, middle, TN) + dot(onehot, low, TN)


vmem = pl.BlockSpec(memory_space=pltpu.VMEM)
smem = pl.BlockSpec(memory_space=pltpu.SMEM)
hbm = pl.BlockSpec(memory_space=pl.ANY)


def outside(arrays):
    return [pltpu.with_memory_space_constraint(a, pltpu.HBM) for a in arrays]


def shape(dims, kind):
    return jax.ShapeDtypeStruct(dims, kind)


def cost(flops, moved, exps=0):
    return pl.CostEstimate(flops=int(flops), bytes_accessed=int(moved), transcendentals=int(exps))


def move(value, target):
    pairs = []
    for i in range(32):
        z, y, x, c = target(i // 8, i // 4 % 2, i // 2 % 2, i % 2)
        pairs.append((i, ((z * 2 + y) * 2 + x) * 2 + c))
    return lax.ppermute(value, ("dp", "tp"), pairs)


def by_z(value, bits):
    return move(value, lambda z, y, x, c: (z ^ bits, y, x, c))


def by_x(value):
    return move(value, lambda z, y, x, c: (z, y, x ^ 1, c))


def by_y(value):
    return move(value, lambda z, y, x, c: (z, y ^ 1, x, c))


def by_xy(value):
    return move(value, lambda z, y, x, c: (z, y ^ 1, x ^ 1, c))


def split_yx(value):
    return move(value, lambda z, y, x, c: (z, y ^ 1, x, c) if c == 0 else (z, y, x ^ 1, c))


def across(value):
    axis = "tp"
    size = lax.axis_size(axis)
    return lax.ppermute(value, axis, [(i, i ^ 1) for i in range(size)])


def stack(pieces):
    return jnp.concatenate(pieces, 0)


def tie(value, *deps):
    return lax.optimization_barrier((value,) + deps)[0]


def by_core(even, odd):
    return jnp.where(lax.axis_index("tp") % 2 == 0, even, odd)


def places(rows):
    here = lax.axis_index("dp")
    slots = jnp.arange(8, dtype=jnp.int32)
    return (((here // 2) ^ (slots % 4)) * 2 + ((here % 2) ^ (slots // 4))) * rows


def column_plan(which, dy, block, lane, rows, sub=0, subs=1):
    return [(which, (j * subs + sub) * rows, rows, dy * 4 + j, block, lane) for j in range(4)]


def quad_plan(which, z, rows, dx, block, lane):
    return [(which, (dx + 2 * dy) * rows, rows, dy * 4 + z, block, lane) for dy in range(2)]


def on_device(
    tokens, prompt, qkv_weight, out_weight, up_weight, down_weight, gain_one, gain_two, segment_ids, pad_flags, cotangent
):
    dp, tp = lax.axis_size("dp"), lax.axis_size("tp")
    tok_dev, width = tokens.shape
    row_count, seq_len = segment_ids.shape
    count = tok_dev + HALO
    rows = qkv_weight.shape[0]
    inner = qkv_weight.shape[2]
    hidden = up_weight.shape[1]
    rank = lax.axis_index("tp")
    core = rank % 2
    row = rank // 2

    shard_a = jnp.concatenate([qkv_weight.reshape(rows, 3 * inner), out_weight.T], axis=1)
    shard_d = down_weight.T
    half = hidden // 2
    up_one, up_two = up_weight[:, :half], up_weight[:, half:]
    down_one, down_two = shard_d[:, :half], shard_d[:, half:]

    if dp == 8:
        a_one, a_two = by_z(shard_a, 1), by_z(shard_a, 2)
        d_x, d_y = by_x(down_two), by_y(down_two)
        a_three = by_z(a_two, 1)
        segment_ids, pad_flags = lax.optimization_barrier((segment_ids, pad_flags, a_two))[:2]

    sent = (1 - core) * (tok_dev - HALO)
    both = stack(
        [
            lax.dynamic_slice_in_dim(tokens, sent, HALO, 0),
            lax.dynamic_slice_in_dim(cotangent, sent, HALO, 0),
        ]
    )
    both = across(both)
    main, side = HALO * core, tok_dev * (1 - core)

    first = core * (seq_len - count)
    seg = lax.dynamic_slice(segment_ids, (row, first), (1, count))
    pad = lax.dynamic_slice(pad_flags, (row, first), (1, count))
    position = jnp.arange(count, dtype=jnp.int32)[None, :]
    live = pad == 0
    index = jnp.full((1, count), -1, jnp.int32)
    begins, keys = [], []
    for s in range(2):
        own = live & (seg == 2 * core + s)
        begin = jnp.min(jnp.where(own, position, count))
        offset = position - begin
        index = jnp.where(own & (offset >= 1) & (offset <= PROMPTS), offset - 1, index)
        begins.append(jnp.minimum(begin, count - KEYS))
        keys.append(lax.dynamic_slice(jnp.where(own, seg, -1), (0, begins[s]), (1, KEYS)))
    column = lambda r: r.reshape(r.shape[1], 1)
    index_col = column(index)
    lows = [b // SLACK * SLACK for b in begins]
    shifts = [b - a for a, b in zip(lows, begins)]
    back_shifts = [(KEYS + SLACK - b) % (KEYS + SLACK) for b in shifts]
    place = jnp.stack([main, side] + lows + shifts + back_shifts).astype(jnp.int32)

    gain_one, gain_two = gain_one[None, :], gain_two[None, :]
    limit = lambda mib: pltpu.CompilerParams(vmem_limit_bytes=mib << 20)
    act = count * width
    mac = 2 * act * width
    start, normed, cot = pl.pallas_call(
        enter_kernel,
        name="enter",
        in_specs=[smem] + [vmem] * 7,
        out_specs=[vmem] * 3,
        out_shape=[pltpu.HBM((count, width), bf16)] * 3,
        cost_estimate=cost(2 * act * 64, 10 * act),
        compiler_params=limit(12),
    )(place, tokens, both[:HALO], cotangent, both[HALO:], prompt, index_col, gain_one)

    blocks = tp
    heads = width // HD
    dma = pltpu.SemaphoreType.DMA
    pair_flops = 2 * 2 * WIN * KEYS * HD * heads

    def attend(plan, arrays):
        return pl.pallas_call(
            functools.partial(attend_kernel, plan),
            name="attend",
            in_specs=[smem] * 2 + [hbm] * 2 + [vmem] * 4 + [hbm] * len(arrays),
            out_specs=[vmem] * 4,
            out_shape=[
                shape((count, width), f32),
                shape((count, width), bf16),
                pltpu.HBM((blocks, count, inner), bf16),
                pltpu.HBM((blocks, 2, KEYS, 2 * inner), bf16),
            ],
            scratch_shapes=[
                pltpu.VMEM((blocks, width, width), bf16),
                pltpu.VMEM((2, WIN, KEYS), f32),
                pltpu.VMEM((count, inner), bf16),
                pltpu.VMEM((count + SLACK, 2 * inner), f32),
                pltpu.VMEM((count, width), bf16),
                pltpu.VMEM((count, width), bf16),
                dma((blocks,)),
                dma((2,)),
            ],
            cost_estimate=cost(4 * mac + 2 * pair_flops, 8 * width * width + 16 * act, 2 * WIN * KEYS * heads),
            compiler_params=limit(24),
        )(place, table, *outside([normed, start]), gain_two, column(seg), *keys, *outside(arrays))

    def mlp(plans, arrays, total, gsum, size, last):
        outs = [shape((count, width), f32)] * 2
        if last:
            outs = [shape((count, width), bf16), shape((count, width), f32), shape((count, width), bf16)]
        sums = [pltpu.VMEM((count, width), f32)] * 2 if last else []
        return pl.pallas_call(
            functools.partial(mlp_kernel, plans, last),
            name="mlp_last" if last else "mlp",
            in_specs=[smem] + [vmem] * 6 + [hbm] * len(arrays),
            out_specs=[vmem] * len(outs),
            out_shape=outs,
            scratch_shapes=sums + [pltpu.VMEM((size, width, width), bf16)] * 2 + [dma((2, size))],
            cost_estimate=cost(4 * size * mac, 4 * size * width * width + 20 * act, 2 * size * act),
            compiler_params=limit(32 if last else 24),
        )(table, normed_two, cot, total, gsum, after, gain_two, *outside(arrays))

    if dp == 8:
        table = places(rows)
        m_own = stack([up_one, down_one, up_two])
        a_col = stack([shard_a, a_one, a_two, a_three])
        a_col, m_own, d_x, d_y = lax.optimization_barrier((a_col, m_own, d_x, d_y, normed))[:4]
        a_x, a_y = by_x(a_col), by_y(a_col)
        m_one, m_two = by_z(m_own, 1), by_z(m_own, 2)
        d_diag = split_yx(by_core(d_x, d_y))
        a_diag = split_yx(tie(by_core(a_x, a_y), m_one, m_two, d_diag))
        m_three = by_z(m_two, 1)
        a_pairs = [(v, across(v)) for v in (a_col, a_x, a_y, a_diag)]
        arrays_a, plan_a = [], []
        for which, pair in enumerate(a_pairs):
            for dc, array in enumerate(pair):
                plan_a += column_plan(len(arrays_a), which // 2, (which % 2) * 2 + dc, 0, rows)
                arrays_a.append(array)
        m_col = tie(stack([m_own, m_one, m_two, m_three]), a_diag)
        d_quad = tie(stack([down_two, d_x, d_y, d_diag]), a_diag)
        m_x, m_y = by_x(m_col), by_y(m_col)
        d_one, d_two = by_z(d_quad, 1), by_z(d_quad, 2)
        arrays_a[0] = tie(arrays_a[0], m_col, d_quad)
        after, normed_two, q_all, kv_all = attend(plan_a, arrays_a)
        m_x, m_y, d_one, d_two, normed_two = lax.optimization_barrier((m_x, m_y, d_one, d_two, normed_two))
        m_diag = split_yx(by_core(m_x, m_y))
        d_three = by_z(d_two, 1)
        def plan(dx, second, block):
            near = [4 * dx + k for k in range(4)]
            ups = [e for k in range(4) for e in column_plan(near[k], k // 2, block, (k % 2) * half, rows, 2 * second, 3)]
            if second:
                downs = [e for k in range(8) for e in quad_plan(8 + k, k // 2, rows, dx, block, (k % 2) * half)]
            else:
                downs = [e for k in range(4) for e in column_plan(near[k], k // 2, block, (k % 2) * half, rows, 1, 3)]
            return ups, downs

        near = [m_col, across(m_col), m_y, across(m_y)]
        total, gsum = mlp(plan(0, 0, 0), near, after, after, 1, False)
        m_diag, d_three = lax.optimization_barrier((m_diag, d_three, gsum))[:2]
        far = [v for k in (m_x, m_diag, d_quad, d_one, d_two, d_three) for v in (k, across(k))]
        plans = [sum(kind, []) for kind in zip(*(plan(*k) for k in ((0, 1, 0), (1, 0, 1), (1, 1, 2))))]
        output, grad_after, branch = mlp(plans, near + far, total, gsum, 3, True)
    else:
        table = jnp.zeros((8,), jnp.int32)

        def whole(shard):
            return lax.all_gather(lax.all_gather(shard, "dp", axis=0, tiled=True), "tp", axis=0, tiled=True)

        arrays_a, plan_a = [whole(shard_a)], [(0, t * width, width, 0, t, 0) for t in range(tp)]
        after, normed_two, q_all, kv_all = attend(plan_a, arrays_a)
        pairs = [whole(up_one), whole(down_one), whole(up_two), whole(down_two)]

        def plan(k, block, kind):
            which = k // 2 * 2 + kind
            return [(which, (k % 2 * 2 + dc) * width, width, 0, block, dc * half) for dc in range(2)]

        total, gsum = mlp([plan(0, 0, kind) for kind in range(2)], pairs[:2], after, after, 1, False)
        plans = [[e for k in (1, 2, 3) for e in plan(k, k - 1, kind)] for kind in range(2)]
        output, grad_after, branch = mlp(plans, pairs, total, gsum, 3, True)

    grad_tok, grad_prm = pl.pallas_call(
        functools.partial(back_kernel, plan_a),
        name="back",
        in_specs=[smem] * 2 + [vmem] * 10 + [hbm] * len(arrays_a),
        out_specs=[vmem] * 2,
        out_shape=[shape((count, width), bf16), shape((64, width), f32)],
        scratch_shapes=[
            pltpu.VMEM((blocks, width, width), bf16),
            pltpu.VMEM((2, KEYS, WIN), f32),
            pltpu.VMEM((count, inner), bf16),
            pltpu.VMEM((count + SLACK, 2 * inner), f32),
            pltpu.VMEM((2, KEYS + SLACK, 2 * inner), f32),
            pltpu.VMEM((count, 3 * inner), bf16),
            pltpu.VMEM((count, width), f32),
            dma((blocks,)),
        ],
        cost_estimate=cost(4 * mac + 5 * pair_flops, 8 * width * width + 16 * act, 2 * WIN * KEYS * heads),
        compiler_params=limit(32),
    )(
        place, table, branch, grad_after, start, q_all, kv_all, gain_one, seg, column(keys[0]), column(keys[1]), index_col,
        *outside(arrays_a),
    )

    mine = lax.dynamic_slice_in_dim(column(seg), main + sent, HALO, 0) // 2 == core

    def settle(window):
        theirs = across(lax.dynamic_slice_in_dim(window, side, HALO, 0))
        own = lax.dynamic_slice_in_dim(window, main, tok_dev, 0)
        kept = lax.dynamic_slice_in_dim(own, sent, HALO, 0)
        return lax.dynamic_update_slice_in_dim(own, jnp.where(mine, kept, theirs), sent, 0)

    prm = grad_prm[:PROMPTS]
    if dp == 8:
        mid = width // 2
        lanes = lambda k: lax.dynamic_slice(prm, (0, k * mid), (PROMPTS, mid)).astype(bf16)
        part = lanes(core).astype(f32) + across(lanes(1 - core)).astype(f32)
        for turns in ((by_x, by_y, by_xy), tuple(functools.partial(by_z, bits=k) for k in (1, 2, 3))):
            sent_prm = part.astype(bf16)
            one, two, three = (turn(sent_prm).astype(f32) for turn in turns)
            part = (sent_prm.astype(f32) + one) + (two + three)
        part = (part / (row_count * dp)).astype(bf16)
        other = across(part)
        grad_prm = jnp.where(core == 0, jnp.concatenate([part, other], 1), jnp.concatenate([other, part], 1))
    else:
        grad_prm = (lax.psum(prm, ("dp", "tp")) / (row_count * dp)).astype(bf16)
    return (settle(output), settle(grad_tok), grad_prm)


def solution(mesh):
    return jax.shard_map(
        on_device,
        mesh=mesh,
        in_specs=(
            P(("dp", "tp"), None),
            P(),
            P("dp", None, "tp"),
            P("tp", "dp"),
            P("dp", "tp"),
            P("tp", "dp"),
            P(),
            P(),
            P("dp", None),
            P("dp", None),
            P(("dp", "tp"), None),
        ),
        out_specs=(P(("dp", "tp"), None), P(("dp", "tp"), None), P()),
        check_vma=False,
    )
```

```python
import functools

import jax
import jax.numpy as jnp
from jax import lax
from jax.experimental import pallas as pl
from jax.experimental.pallas import tpu as pltpu
from jax.sharding import PartitionSpec as P

HD = 64
PROMPTS = 50
HALO = 32
WIN = 304
KEYS = 256
SLACK = 8
NT = (((1,), (1,)), ((), ()))
NN = (((1,), (0,)), ((), ()))
TN = (((0,), (0,)), ((), ()))
eps = 1e-6
fill = -1e30
floor = -1e29
bf16 = jnp.bfloat16
f32 = jnp.float32


def dot(a, b, dims=NN):
    return lax.dot_general(a, b, dims, preferred_element_type=f32)


def norm_parts(values):
    centred = values - jnp.mean(values, axis=-1, keepdims=True)
    scale = lax.rsqrt(jnp.mean(centred * centred, axis=-1, keepdims=True) + eps)
    return centred * scale, scale


def norm_back(unit, scale, grad, gain):
    u = grad * gain
    return scale * (
        u - jnp.mean(u, axis=-1, keepdims=True) - unit * jnp.mean(u * unit, axis=-1, keepdims=True)
    )


def window_starts(count):
    return (0, count - WIN)


def join_windows(first, second, count):
    low = count - WIN
    return jnp.concatenate([first[:low], first[low:] + second[: WIN - low], second[WIN - low :]], 0)


def fetch(plan, table, refs, buf, sems):
    for which, source, rows, slot, block, lane in plan:
        lanes = refs[which].shape[1]
        pltpu.make_async_copy(
            refs[which].at[pl.ds(source, rows)],
            buf.at[block, pl.ds(pl.multiple_of(table[slot], 16), rows), pl.ds(lane, lanes)],
            sems.at[block],
        ).start()


def arrive(buf, sems, block):
    pltpu.make_async_copy(buf.at[block], buf.at[block], sems.at[block]).wait()


def shifted_in(wide, place, s):
    low = pl.multiple_of(place[2 + s], SLACK)
    value = wide[pl.ds(low, KEYS + SLACK), :]
    return pltpu.roll(value, place[6 + s], 0)[:KEYS]


def enter_kernel(place, own, own_halo, cot, cot_halo, prompt, index, gain, start, normed, cot_out):
    main = pl.multiple_of(place[0], HALO)
    side = pl.multiple_of(place[1], HALO)
    rows = own.shape[0]
    start[pl.ds(main, rows), :] = own[...]
    start[pl.ds(side, HALO), :] = own_halo[...]
    cot_out[pl.ds(main, rows), :] = cot[...]
    cot_out[pl.ds(side, HALO), :] = cot_halo[...]
    idx = index[...]
    lanes = lax.broadcasted_iota(jnp.int32, (idx.shape[0], PROMPTS), 1)
    onehot = (idx == lanes).astype(f32).astype(bf16)
    picked = dot(onehot, prompt[...])
    value = jnp.where(idx >= 0, picked, start[...].astype(f32))
    start[...] = value.astype(bf16)
    unit, _ = norm_parts(value)
    normed[...] = (unit * gain[...].astype(f32)).astype(bf16)


def attend_kernel(plan, place, table, normed, start, gain, qseg, krow_a, krow_b, *rest):
    n = len(rest) - 12
    refs, (after, normed_two, q_out, kv_out, buf, bias, mix, wide, normed_in, start_in, sems, own_sems) = rest[:n], rest[n:]
    count = normed.shape[0]
    inner = q_out.shape[2]
    heads = inner // HD
    own = [
        pltpu.make_async_copy(normed, normed_in, own_sems.at[0]),
        pltpu.make_async_copy(start, start_in, own_sems.at[1]),
    ]
    for copy in own:
        copy.start()
    fetch(plan, table, refs, buf, sems)
    starts = window_starts(count)
    for s, krow in enumerate((krow_a, krow_b)):
        bias[s] = jnp.where(qseg[starts[s] : starts[s] + WIN, :] == krow[...], 0.0, fill)
    wide[count:] = jnp.zeros_like(wide[count:])
    for copy in own:
        copy.wait()
    after[...] = start_in[...].astype(f32)

    def step(block, carry):
        arrive(buf, sems, block)
        weight = buf.at[block]
        both = dot(normed_in[...], weight[:, : 3 * inner])
        q_all = both[:, :inner].astype(bf16) * bf16(HD**-0.5)
        q_out[block] = q_all
        wide[:count] = both[:, inner:]
        pairs = [shifted_in(wide, place, s).astype(bf16) for s in range(2)]
        for s in range(2):
            kv_out[block, s] = pairs[s]
        for h in range(heads):
            parts = []
            for s in range(2):
                q = q_all[starts[s] : starts[s] + WIN, h * HD : (h + 1) * HD]
                k = pairs[s][:, h * HD : (h + 1) * HD]
                v = pairs[s][:, inner + h * HD : inner + (h + 1) * HD]
                scores = dot(q, k, NT) + bias[s]
                top = jnp.maximum(jnp.max(scores, axis=-1, keepdims=True), floor)
                weights = jnp.exp(scores - top)
                total = jnp.maximum(jnp.sum(weights, axis=-1, keepdims=True), 1e-30)
                probs = (weights * (1.0 / total)).astype(bf16)
                parts.append(dot(probs, v))
            mix[:, h * HD : (h + 1) * HD] = join_windows(parts[0], parts[1], count).astype(bf16)
        after[...] += dot(mix[...], weight[:, 3 * inner :], NT)
        return carry

    lax.fori_loop(0, buf.shape[0], step, 0)
    unit, _ = norm_parts(after[...])
    normed_two[...] = (unit * gain[...].astype(f32)).astype(bf16)


def mlp_kernel(plans, last, table, normed_two, gain, *rest):
    n = len(rest) - (15 if last else 12)
    held, refs, rest = rest[: 4 if last else 2], rest[4 if last else 2 :][:n], rest[4 if last else 2 :][n:]
    if last:
        output, grad_after, branch, cot, after, total, gsum, up, down, sems, own_sems = rest
    else:
        total_out, gsum_out, cot, after, total, gsum, up, down, sems, own_sems = rest
    fetch(plans[0], table, refs, up, sems.at[0])
    fetch(plans[1], table, refs, down, sems.at[1])
    own = [
        pltpu.make_async_copy(source, place, own_sems.at[k])
        for k, (source, place) in enumerate(zip(held, (cot, after, total, gsum)))
    ]
    for copy in own:
        copy.start()

    def step(block, carry):
        arrive(up, sems.at[0], block)
        pre = dot(normed_two[...], up[block])
        cdf = 0.5 + 0.5 * lax.erf(pre * (0.5**0.5))
        slope = cdf + pre * (jnp.exp(-0.5 * pre * pre) * 0.3989422804014327)
        act = (pre * cdf).astype(bf16)
        arrive(down, sems.at[1], block)
        if isinstance(block, int):
            own[0].wait()
        back = dot(cot[...], down[block])
        grad_pre = (back * slope).astype(bf16)
        if last:
            if isinstance(block, int):
                own[2].wait()
                own[3].wait()
            total[...] += dot(act, down[block], NT)
            gsum[...] += dot(grad_pre, up[block], NT)
        else:
            own[1].wait()
            total[...] = after[...] + dot(act, down[block], NT)
            give = pltpu.make_async_copy(total, total_out, own_sems.at[0])
            give.start()
            gsum[...] = dot(grad_pre, up[block], NT)
            give_more = pltpu.make_async_copy(gsum, gsum_out, own_sems.at[1])
            give_more.start()
            give.wait()
            give_more.wait()
        return carry

    step(0, 0)
    if last:
        lax.fori_loop(1, up.shape[0], step, 0)
        own[1].wait()
        output[...] = total[...].astype(bf16)
        unit, scale = norm_parts(after[...])
        grad = cot[...].astype(f32) + norm_back(unit, scale, gsum[...], gain[...].astype(f32))
        grad_after[...] = grad
        branch[...] = grad.astype(bf16)


def back_kernel(plan, place, table, branch, grad_after, start, q_all, kv_all, gain, qrow, kcol_a, kcol_b, index, *rest):
    n = len(rest) - 10
    refs, (grad_tok, grad_prm, buf, bias, gmix, gq, gkv, gqkv, gsum, sems) = rest[:n], rest[n:]
    count = branch.shape[0]
    inner = q_all.shape[2]
    heads = inner // HD
    fetch(plan, table, refs, buf, sems)
    starts = window_starts(count)
    for s, kcol in enumerate((kcol_a, kcol_b)):
        bias[s] = jnp.where(kcol[...] == qrow[...][:, starts[s] : starts[s] + WIN], 0.0, fill)
    gsum[...] = jnp.zeros_like(gsum)
    gkv[...] = jnp.zeros_like(gkv)

    def step(block, carry):
        arrive(buf, sems, block)
        weight = buf.at[block]
        gmix[...] = dot(branch[...], weight[:, 3 * inner :]).astype(bf16)
        for h in range(heads):
            cols = slice(h * HD, (h + 1) * HD)
            late = slice(inner + h * HD, inner + (h + 1) * HD)
            parts = []
            for s in range(2):
                rows = slice(starts[s], starts[s] + WIN)
                q = q_all[block, rows, cols]
                k = kv_all[block, s, :, cols]
                v = kv_all[block, s, :, late]
                g = gmix[rows, cols]
                scores = dot(k, q, NT) + bias[s]
                top = jnp.maximum(jnp.max(scores, axis=0, keepdims=True), floor)
                weights = jnp.exp(scores - top)
                total = jnp.maximum(jnp.sum(weights, axis=0, keepdims=True), 1e-30)
                probs = weights * (1.0 / total)
                grad_probs = dot(v, g, NT)
                centre = jnp.sum(grad_probs * probs, axis=0, keepdims=True)
                grad_scores = (probs * (grad_probs - centre)).astype(bf16)
                parts.append(dot(grad_scores, k * bf16(HD**-0.5), TN))
                gkv[s, :KEYS, cols] = dot(grad_scores, q)
                gkv[s, :KEYS, late] = dot(probs.astype(bf16), g)
            gqkv[:, cols] = join_windows(parts[0], parts[1], count).astype(bf16)
        gq[...] = jnp.zeros_like(gq)
        for s in range(2):
            low = pl.multiple_of(place[2 + s], SLACK)
            gq[pl.ds(low, KEYS + SLACK), :] += pltpu.roll(gkv[s], place[4 + s], 0)
        gqkv[:, inner:] = gq[:count].astype(bf16)
        gsum[...] += dot(gqkv[...], weight[:, : 3 * inner], NT)
        return carry

    lax.fori_loop(0, buf.shape[0], step, 0)
    unit, scale = norm_parts(start[...].astype(f32))
    grad = grad_after[...] + norm_back(unit, scale, gsum[...], gain[...].astype(f32))
    idx = index[...]
    grad_tok[...] = jnp.where(idx >= 0, 0.0, grad).astype(bf16)
    lanes = lax.broadcasted_iota(jnp.int32, (count, grad_prm.shape[0]), 1)
    onehot = (idx == lanes).astype(f32).astype(bf16)
    high = grad.astype(bf16)
    rest_one = grad - high.astype(f32)
    middle = rest_one.astype(bf16)
    low = (rest_one - middle.astype(f32)).astype(bf16)
    grad_prm[...] = dot(onehot, high, TN) + dot(onehot, middle, TN) + dot(onehot, low, TN)


vmem = pl.BlockSpec(memory_space=pltpu.VMEM)
smem = pl.BlockSpec(memory_space=pltpu.SMEM)
hbm = pl.BlockSpec(memory_space=pl.ANY)


def outside(arrays):
    return [pltpu.with_memory_space_constraint(a, pltpu.HBM) for a in arrays]


def shape(dims, kind):
    return jax.ShapeDtypeStruct(dims, kind)


def cost(flops, moved, exps=0):
    return pl.CostEstimate(flops=int(flops), bytes_accessed=int(moved), transcendentals=int(exps))


def move(value, target):
    pairs = []
    for i in range(32):
        z, y, x, c = target(i // 8, i // 4 % 2, i // 2 % 2, i % 2)
        pairs.append((i, ((z * 2 + y) * 2 + x) * 2 + c))
    return lax.ppermute(value, ("dp", "tp"), pairs)


def by_z(value, bits):
    return move(value, lambda z, y, x, c: (z ^ bits, y, x, c))


def by_x(value):
    return move(value, lambda z, y, x, c: (z, y, x ^ 1, c))


def by_y(value):
    return move(value, lambda z, y, x, c: (z, y ^ 1, x, c))


def by_xy(value):
    return move(value, lambda z, y, x, c: (z, y ^ 1, x ^ 1, c))


def split_yx(value):
    return move(value, lambda z, y, x, c: (z, y ^ 1, x, c) if c == 0 else (z, y, x ^ 1, c))


def across(value):
    axis = "tp"
    size = lax.axis_size(axis)
    return lax.ppermute(value, axis, [(i, i ^ 1) for i in range(size)])


def stack(pieces):
    return jnp.concatenate(pieces, 0)


def tie(value, *deps):
    return lax.optimization_barrier((value,) + deps)[0]


def by_core(even, odd):
    return jnp.where(lax.axis_index("tp") % 2 == 0, even, odd)


def places(rows):
    here = lax.axis_index("dp")
    slots = jnp.arange(8, dtype=jnp.int32)
    return (((here // 2) ^ (slots % 4)) * 2 + ((here % 2) ^ (slots // 4))) * rows


def column_plan(which, dy, block, lane, rows, sub=0, subs=1):
    return [(which, (j * subs + sub) * rows, rows, dy * 4 + j, block, lane) for j in range(4)]


def quad_plan(which, z, rows, dx, block, lane):
    return [(which, (dx + 2 * dy) * rows, rows, dy * 4 + z, block, lane) for dy in range(2)]


def on_device(
    tokens, prompt, qkv_weight, out_weight, up_weight, down_weight, gain_one, gain_two, segment_ids, pad_flags, cotangent
):
    dp, tp = lax.axis_size("dp"), lax.axis_size("tp")
    tok_dev, width = tokens.shape
    row_count, seq_len = segment_ids.shape
    count = tok_dev + HALO
    rows = qkv_weight.shape[0]
    inner = qkv_weight.shape[2]
    hidden = up_weight.shape[1]
    rank = lax.axis_index("tp")
    core = rank % 2
    row = rank // 2

    shard_a = jnp.concatenate([qkv_weight.reshape(rows, 3 * inner), out_weight.T], axis=1)
    shard_d = down_weight.T
    half = hidden // 2
    up_one, up_two = up_weight[:, :half], up_weight[:, half:]
    down_one, down_two = shard_d[:, :half], shard_d[:, half:]

    if dp == 8:
        a_one, a_two = by_z(shard_a, 1), by_z(shard_a, 2)
        d_x, d_y = by_x(down_two), by_y(down_two)
        a_three = by_z(a_two, 1)
        segment_ids, pad_flags = lax.optimization_barrier((segment_ids, pad_flags, a_two))[:2]
        prompt = tie(prompt, a_three)

    sent = (1 - core) * (tok_dev - HALO)
    both = stack(
        [
            lax.dynamic_slice_in_dim(tokens, sent, HALO, 0),
            lax.dynamic_slice_in_dim(cotangent, sent, HALO, 0),
        ]
    )
    both = across(both)
    main, side = HALO * core, tok_dev * (1 - core)

    first = core * (seq_len - count)
    seg = lax.dynamic_slice(segment_ids, (row, first), (1, count))
    pad = lax.dynamic_slice(pad_flags, (row, first), (1, count))
    position = jnp.arange(count, dtype=jnp.int32)[None, :]
    live = pad == 0
    index = jnp.full((1, count), -1, jnp.int32)
    begins, keys = [], []
    for s in range(2):
        own = live & (seg == 2 * core + s)
        begin = jnp.min(jnp.where(own, position, count))
        offset = position - begin
        index = jnp.where(own & (offset >= 1) & (offset <= PROMPTS), offset - 1, index)
        begins.append(jnp.minimum(begin, count - KEYS))
        keys.append(lax.dynamic_slice(jnp.where(own, seg, -1), (0, begins[s]), (1, KEYS)))
    column = lambda r: r.reshape(r.shape[1], 1)
    index_col = column(index)
    lows = [b // SLACK * SLACK for b in begins]
    shifts = [b - a for a, b in zip(lows, begins)]
    back_shifts = [(KEYS + SLACK - b) % (KEYS + SLACK) for b in shifts]
    place = jnp.stack([main, side] + lows + shifts + back_shifts).astype(jnp.int32)

    gain_one, gain_two = gain_one[None, :], gain_two[None, :]
    limit = lambda mib: pltpu.CompilerParams(vmem_limit_bytes=mib << 20)
    act = count * width
    mac = 2 * act * width
    start, normed, cot = pl.pallas_call(
        enter_kernel,
        name="enter",
        in_specs=[smem] + [vmem] * 7,
        out_specs=[vmem] * 3,
        out_shape=[pltpu.HBM((count, width), bf16)] * 3,
        cost_estimate=cost(2 * act * 64, 10 * act),
        compiler_params=limit(12),
    )(place, tokens, both[:HALO], cotangent, both[HALO:], prompt, index_col, gain_one)

    blocks = tp
    heads = width // HD
    dma = pltpu.SemaphoreType.DMA
    pair_flops = 2 * 2 * WIN * KEYS * HD * heads

    def attend(plan, arrays):
        return pl.pallas_call(
            functools.partial(attend_kernel, plan),
            name="attend",
            in_specs=[smem] * 2 + [hbm] * 2 + [vmem] * 4 + [hbm] * len(arrays),
            out_specs=[vmem] * 4,
            out_shape=[
                pltpu.HBM((count, width), f32),
                shape((count, width), bf16),
                pltpu.HBM((blocks, count, inner), bf16),
                pltpu.HBM((blocks, 2, KEYS, 2 * inner), bf16),
            ],
            scratch_shapes=[
                pltpu.VMEM((blocks, width, width), bf16),
                pltpu.VMEM((2, WIN, KEYS), f32),
                pltpu.VMEM((count, inner), bf16),
                pltpu.VMEM((count + SLACK, 2 * inner), f32),
                pltpu.VMEM((count, width), bf16),
                pltpu.VMEM((count, width), bf16),
                dma((blocks,)),
                dma((2,)),
            ],
            cost_estimate=cost(4 * mac + 2 * pair_flops, 8 * width * width + 16 * act, 2 * WIN * KEYS * heads),
            compiler_params=limit(24),
        )(place, table, *outside([normed, start]), gain_two, column(seg), *keys, *outside(arrays))

    def mlp(plans, arrays, held, size, last):
        outs = [pltpu.HBM((count, width), f32)] * 2
        if last:
            outs = [shape((count, width), bf16), shape((count, width), f32), shape((count, width), bf16)]
        return pl.pallas_call(
            functools.partial(mlp_kernel, plans, last),
            name="mlp_last" if last else "mlp",
            in_specs=[smem] + [vmem] * 2 + [hbm] * (len(held) + len(arrays)),
            out_specs=[vmem if last else hbm] * len(outs),
            out_shape=outs,
            scratch_shapes=[pltpu.VMEM((count, width), kind) for kind in (bf16, f32, f32, f32)]
            + [pltpu.VMEM((size, width, width), bf16)] * 2
            + [dma((2, size)), dma((len(held),))],
            cost_estimate=cost(4 * size * mac, 4 * size * width * width + 20 * act, 2 * size * act),
            compiler_params=limit(40 if last else 24),
        )(table, normed_two, gain_two, *outside(held), *outside(arrays))

    if dp == 8:
        table = places(rows)
        m_own = stack([up_one, down_one, up_two])
        a_col = stack([shard_a, a_one, a_two, a_three])
        a_col, m_own, d_x, d_y, both, index_col, place, *keys = lax.optimization_barrier(
            (a_col, m_own, d_x, d_y, both, index_col, place, *keys)
        )
        a_x, a_y = by_x(a_col), by_y(a_col)
        m_one, m_two = by_z(m_own, 1), by_z(m_own, 2)
        d_diag = split_yx(tie(by_core(d_x, d_y), a_x))
        a_diag = split_yx(tie(by_core(a_x, a_y), m_one, normed))
        m_three = by_z(m_two, 1)
        a_pairs = [(v, across(v)) for v in (a_col, a_x, a_y, a_diag)]
        arrays_a, plan_a = [], []
        for which, pair in enumerate(a_pairs):
            for dc, array in enumerate(pair):
                plan_a += column_plan(len(arrays_a), which // 2, (which % 2) * 2 + dc, 0, rows)
                arrays_a.append(array)
        m_col = tie(stack([m_own, m_one, m_two, m_three]), a_diag)
        d_quad = tie(stack([down_two, d_x, d_y, d_diag]), a_diag)
        m_x, m_y = by_x(m_col), by_y(m_col)
        d_one, d_two = by_z(d_quad, 1), by_z(d_quad, 2)
        arrays_a[0] = tie(arrays_a[0], m_col, d_quad)
        after, normed_two, q_all, kv_all = attend(plan_a, arrays_a)
        m_x, m_y, d_one, d_two, normed_two = lax.optimization_barrier((m_x, m_y, d_one, d_two, normed_two))
        m_diag = split_yx(by_core(m_x, m_y))
        d_three = by_z(d_two, 1)
        def plan(dx, second, block):
            near = [4 * dx + k for k in range(4)]
            ups = [e for k in range(4) for e in column_plan(near[k], k // 2, block, (k % 2) * half, rows, 2 * second, 3)]
            if second:
                downs = [e for k in range(8) for e in quad_plan(8 + k, k // 2, rows, dx, block, (k % 2) * half)]
            else:
                downs = [e for k in range(4) for e in column_plan(near[k], k // 2, block, (k % 2) * half, rows, 1, 3)]
            return ups, downs

        near = [m_col, across(m_col), m_y, across(m_y)]
        total, gsum = mlp(plan(0, 0, 0), near, [cot, after], 1, False)
        m_diag, d_three = lax.optimization_barrier((m_diag, d_three, gsum))[:2]
        far = [v for k in (m_x, m_diag, d_quad, d_one, d_two, d_three) for v in (k, across(k))]
        plans = [sum(kind, []) for kind in zip(*(plan(*k) for k in ((0, 1, 0), (1, 0, 1), (1, 1, 2))))]
        output, grad_after, branch = mlp(plans, near + far, [cot, after, total, gsum], 3, True)
    else:
        table = jnp.zeros((8,), jnp.int32)

        def whole(shard):
            return lax.all_gather(lax.all_gather(shard, "dp", axis=0, tiled=True), "tp", axis=0, tiled=True)

        arrays_a, plan_a = [whole(shard_a)], [(0, t * width, width, 0, t, 0) for t in range(tp)]
        after, normed_two, q_all, kv_all = attend(plan_a, arrays_a)
        pairs = [whole(up_one), whole(down_one), whole(up_two), whole(down_two)]

        def plan(k, block, kind):
            which = k // 2 * 2 + kind
            return [(which, (k % 2 * 2 + dc) * width, width, 0, block, dc * half) for dc in range(2)]

        total, gsum = mlp([plan(0, 0, kind) for kind in range(2)], pairs[:2], [cot, after], 1, False)
        plans = [[e for k in (1, 2, 3) for e in plan(k, k - 1, kind)] for kind in range(2)]
        output, grad_after, branch = mlp(plans, pairs, [cot, after, total, gsum], 3, True)

    grad_tok, grad_prm = pl.pallas_call(
        functools.partial(back_kernel, plan_a),
        name="back",
        in_specs=[smem] * 2 + [vmem] * 10 + [hbm] * len(arrays_a),
        out_specs=[vmem] * 2,
        out_shape=[shape((count, width), bf16), shape((64, width), f32)],
        scratch_shapes=[
            pltpu.VMEM((blocks, width, width), bf16),
            pltpu.VMEM((2, KEYS, WIN), f32),
            pltpu.VMEM((count, inner), bf16),
            pltpu.VMEM((count + SLACK, 2 * inner), f32),
            pltpu.VMEM((2, KEYS + SLACK, 2 * inner), f32),
            pltpu.VMEM((count, 3 * inner), bf16),
            pltpu.VMEM((count, width), f32),
            dma((blocks,)),
        ],
        cost_estimate=cost(4 * mac + 5 * pair_flops, 8 * width * width + 16 * act, 2 * WIN * KEYS * heads),
        compiler_params=limit(32),
    )(
        place, table, branch, grad_after, start, q_all, kv_all, gain_one, seg, column(keys[0]), column(keys[1]), index_col,
        *outside(arrays_a),
    )

    mine = lax.dynamic_slice_in_dim(column(seg), main + sent, HALO, 0) // 2 == core

    def settle(window):
        theirs = across(lax.dynamic_slice_in_dim(window, side, HALO, 0))
        own = lax.dynamic_slice_in_dim(window, main, tok_dev, 0)
        kept = lax.dynamic_slice_in_dim(own, sent, HALO, 0)
        return lax.dynamic_update_slice_in_dim(own, jnp.where(mine, kept, theirs), sent, 0)

    prm = grad_prm[:PROMPTS]
    if dp == 8:
        mid = width // 2
        lanes = lambda k: lax.dynamic_slice(prm, (0, k * mid), (PROMPTS, mid)).astype(bf16)
        part = lanes(core).astype(f32) + across(lanes(1 - core)).astype(f32)
        for turns in ((by_x, by_y, by_xy), tuple(functools.partial(by_z, bits=k) for k in (1, 2, 3))):
            sent_prm = part.astype(bf16)
            one, two, three = (turn(sent_prm).astype(f32) for turn in turns)
            part = (sent_prm.astype(f32) + one) + (two + three)
        part = (part / (row_count * dp)).astype(bf16)
        other = across(part)
        grad_prm = jnp.where(core == 0, jnp.concatenate([part, other], 1), jnp.concatenate([other, part], 1))
    else:
        grad_prm = (lax.psum(prm, ("dp", "tp")) / (row_count * dp)).astype(bf16)
    return (settle(output), settle(grad_tok), grad_prm)


def solution(mesh):
    return jax.shard_map(
        on_device,
        mesh=mesh,
        in_specs=(
            P(("dp", "tp"), None),
            P(),
            P("dp", None, "tp"),
            P("tp", "dp"),
            P("dp", "tp"),
            P("tp", "dp"),
            P(),
            P(),
            P("dp", None),
            P("dp", None),
            P(("dp", "tp"), None),
        ),
        out_specs=(P(("dp", "tp"), None), P(("dp", "tp"), None), P()),
        check_vma=False,
    )
```

```python
import functools

import jax
import jax.numpy as jnp
from jax import lax
from jax.experimental import pallas as pl
from jax.experimental.pallas import tpu as pltpu
from jax.sharding import PartitionSpec as P

HD = 64
PROMPTS = 50
HALO = 32
WIN = 304
KEYS = 256
SLACK = 8
NT = (((1,), (1,)), ((), ()))
NN = (((1,), (0,)), ((), ()))
TN = (((0,), (0,)), ((), ()))
eps = 1e-6
fill = -1e30
floor = -1e29
bf16 = jnp.bfloat16
f32 = jnp.float32


def dot(a, b, dims=NN):
    return lax.dot_general(a, b, dims, preferred_element_type=f32)


def norm_parts(values):
    centred = values - jnp.mean(values, axis=-1, keepdims=True)
    scale = lax.rsqrt(jnp.mean(centred * centred, axis=-1, keepdims=True) + eps)
    return centred * scale, scale


def norm_back(unit, scale, grad, gain):
    u = grad * gain
    return scale * (
        u - jnp.mean(u, axis=-1, keepdims=True) - unit * jnp.mean(u * unit, axis=-1, keepdims=True)
    )


def window_starts(count):
    return (0, count - WIN)


def join_windows(first, second, count):
    low = count - WIN
    return jnp.concatenate([first[:low], first[low:] + second[: WIN - low], second[WIN - low :]], 0)


def fetch(plan, table, refs, buf, sems, later=False):
    for which, source, rows, slot, block, lane in plan:
        if (block > 0) != later:
            continue
        lanes = refs[which].shape[1]
        pltpu.make_async_copy(
            refs[which].at[pl.ds(source, rows)],
            buf.at[block, pl.ds(pl.multiple_of(table[slot], 16), rows), pl.ds(lane, lanes)],
            sems.at[block],
        ).start()


def arrive(buf, sems, block):
    pltpu.make_async_copy(buf.at[block], buf.at[block], sems.at[block]).wait()


def shifted_in(wide, place, s):
    low = pl.multiple_of(place[2 + s], SLACK)
    value = wide[pl.ds(low, KEYS + SLACK), :]
    return pltpu.roll(value, place[6 + s], 0)[:KEYS]


def enter_kernel(place, own, own_halo, cot, cot_halo, prompt, index, gain, start, normed, cot_out):
    main = pl.multiple_of(place[0], HALO)
    side = pl.multiple_of(place[1], HALO)
    rows = own.shape[0]
    start[pl.ds(main, rows), :] = own[...]
    start[pl.ds(side, HALO), :] = own_halo[...]
    cot_out[pl.ds(main, rows), :] = cot[...]
    cot_out[pl.ds(side, HALO), :] = cot_halo[...]
    idx = index[...]
    lanes = lax.broadcasted_iota(jnp.int32, (idx.shape[0], PROMPTS), 1)
    onehot = (idx == lanes).astype(f32).astype(bf16)
    picked = dot(onehot, prompt[...])
    value = jnp.where(idx >= 0, picked, start[...].astype(f32))
    start[...] = value.astype(bf16)
    unit, _ = norm_parts(value)
    normed[...] = (unit * gain[...].astype(f32)).astype(bf16)


def attend_kernel(plan, place, table, normed, start, gain, qseg, krow_a, krow_b, *rest):
    n = len(rest) - 15
    refs, rest = rest[:n], rest[n:]
    after_out, normed_two, q_out, kv_out, buf, bias, mix, wide, normed_in, start_in, *rest = rest
    after, q_kept, kv_kept, sems, own_sems = rest
    count = normed.shape[0]
    inner = q_out.shape[2]
    heads = inner // HD
    own = [
        pltpu.make_async_copy(normed, normed_in, own_sems.at[0]),
        pltpu.make_async_copy(start, start_in, own_sems.at[1]),
    ]
    own[0].start()
    fetch(plan, table, refs, buf, sems)
    own[1].start()
    starts = window_starts(count)
    for s, krow in enumerate((krow_a, krow_b)):
        bias[s] = jnp.where(qseg[starts[s] : starts[s] + WIN, :] == krow[...], 0.0, fill)
    wide[count:] = jnp.zeros_like(wide[count:])
    for copy in own:
        copy.wait()
    after[...] = start_in[...].astype(f32)
    arrive(buf, sems, 0)
    fetch(plan, table, refs, buf, sems, later=True)

    def step(block, carry):
        @pl.when(block > 0)
        def _():
            arrive(buf, sems, block)

        weight = buf.at[block]
        both = dot(normed_in[...], weight[:, : 3 * inner])
        q_all = both[:, :inner].astype(bf16) * bf16(HD**-0.5)
        q_kept[block] = q_all
        wide[:count] = both[:, inner:]
        pairs = [shifted_in(wide, place, s).astype(bf16) for s in range(2)]
        for s in range(2):
            kv_kept[block, s] = pairs[s]
        pltpu.make_async_copy(q_kept.at[block], q_out.at[block], own_sems.at[2]).start()
        pltpu.make_async_copy(kv_kept.at[block], kv_out.at[block], own_sems.at[3]).start()
        for h in range(heads):
            parts = []
            for s in range(2):
                q = q_all[starts[s] : starts[s] + WIN, h * HD : (h + 1) * HD]
                k = pairs[s][:, h * HD : (h + 1) * HD]
                v = pairs[s][:, inner + h * HD : inner + (h + 1) * HD]
                scores = dot(q, k, NT) + bias[s]
                top = jnp.maximum(jnp.max(scores, axis=-1, keepdims=True), floor)
                weights = jnp.exp(scores - top)
                total = jnp.maximum(jnp.sum(weights, axis=-1, keepdims=True), 1e-30)
                probs = (weights * (1.0 / total)).astype(bf16)
                parts.append(dot(probs, v))
            mix[:, h * HD : (h + 1) * HD] = join_windows(parts[0], parts[1], count).astype(bf16)
        after[...] += dot(mix[...], weight[:, 3 * inner :], NT)
        return carry

    lax.fori_loop(0, buf.shape[0], step, 0)
    give = pltpu.make_async_copy(after, after_out, own_sems.at[0])
    give.start()
    unit, _ = norm_parts(after[...])
    normed_two[...] = (unit * gain[...].astype(f32)).astype(bf16)
    give.wait()
    pltpu.make_async_copy(q_kept, q_out, own_sems.at[2]).wait()
    pltpu.make_async_copy(kv_kept, kv_out, own_sems.at[3]).wait()


def mlp_kernel(plans, last, table, normed_two, gain, *rest):
    n = len(rest) - (15 if last else 12)
    held, refs, rest = rest[: 4 if last else 2], rest[4 if last else 2 :][:n], rest[4 if last else 2 :][n:]
    if last:
        output, grad_after, branch, cot, after, total, gsum, up, down, sems, own_sems = rest
    else:
        total_out, gsum_out, cot, after, total, gsum, up, down, sems, own_sems = rest
    for later in (False, True):
        fetch(plans[0], table, refs, up, sems.at[0], later)
        fetch(plans[1], table, refs, down, sems.at[1], later)
    own = [
        pltpu.make_async_copy(source, place, own_sems.at[k])
        for k, (source, place) in enumerate(zip(held, (cot, after, total, gsum)))
    ]
    for copy in own:
        copy.start()

    def step(block, carry):
        arrive(up, sems.at[0], block)
        pre = dot(normed_two[...], up[block])
        cdf = 0.5 + 0.5 * lax.erf(pre * (0.5**0.5))
        slope = cdf + pre * (jnp.exp(-0.5 * pre * pre) * 0.3989422804014327)
        act = (pre * cdf).astype(bf16)
        arrive(down, sems.at[1], block)
        if isinstance(block, int):
            own[0].wait()
        back = dot(cot[...], down[block])
        grad_pre = (back * slope).astype(bf16)
        if last:
            if isinstance(block, int):
                own[2].wait()
                own[3].wait()
            total[...] += dot(act, down[block], NT)
            gsum[...] += dot(grad_pre, up[block], NT)
        else:
            own[1].wait()
            total[...] = after[...] + dot(act, down[block], NT)
            give = pltpu.make_async_copy(total, total_out, own_sems.at[0])
            give.start()
            gsum[...] = dot(grad_pre, up[block], NT)
            give_more = pltpu.make_async_copy(gsum, gsum_out, own_sems.at[1])
            give_more.start()
            give.wait()
            give_more.wait()
        return carry

    step(0, 0)
    if last:
        lax.fori_loop(1, up.shape[0], step, 0)
        own[1].wait()
        output[...] = total[...].astype(bf16)
        unit, scale = norm_parts(after[...])
        grad = cot[...].astype(f32) + norm_back(unit, scale, gsum[...], gain[...].astype(f32))
        grad_after[...] = grad
        branch[...] = grad.astype(bf16)


def back_kernel(plan, place, table, branch, grad_after, start, q_all, kv_all, gain, qrow, kcol_a, kcol_b, index, *rest):
    n = len(rest) - 10
    refs, (grad_tok, grad_prm, buf, bias, gmix, gq, gkv, gqkv, gsum, sems) = rest[:n], rest[n:]
    count = branch.shape[0]
    inner = q_all.shape[2]
    heads = inner // HD
    fetch(plan, table, refs, buf, sems)
    starts = window_starts(count)
    for s, kcol in enumerate((kcol_a, kcol_b)):
        bias[s] = jnp.where(kcol[...] == qrow[...][:, starts[s] : starts[s] + WIN], 0.0, fill)
    gsum[...] = jnp.zeros_like(gsum)
    gkv[...] = jnp.zeros_like(gkv)
    arrive(buf, sems, 0)
    fetch(plan, table, refs, buf, sems, later=True)

    def step(block, carry):
        @pl.when(block > 0)
        def _():
            arrive(buf, sems, block)

        weight = buf.at[block]
        gmix[...] = dot(branch[...], weight[:, 3 * inner :]).astype(bf16)
        for h in range(heads):
            cols = slice(h * HD, (h + 1) * HD)
            late = slice(inner + h * HD, inner + (h + 1) * HD)
            parts = []
            for s in range(2):
                rows = slice(starts[s], starts[s] + WIN)
                q = q_all[block, rows, cols]
                k = kv_all[block, s, :, cols]
                v = kv_all[block, s, :, late]
                g = gmix[rows, cols]
                scores = dot(k, q, NT) + bias[s]
                top = jnp.maximum(jnp.max(scores, axis=0, keepdims=True), floor)
                weights = jnp.exp(scores - top)
                total = jnp.maximum(jnp.sum(weights, axis=0, keepdims=True), 1e-30)
                probs = weights * (1.0 / total)
                grad_probs = dot(v, g, NT)
                centre = jnp.sum(grad_probs * probs, axis=0, keepdims=True)
                grad_scores = (probs * (grad_probs - centre)).astype(bf16)
                parts.append(dot(grad_scores, k * bf16(HD**-0.5), TN))
                gkv[s, :KEYS, cols] = dot(grad_scores, q)
                gkv[s, :KEYS, late] = dot(probs.astype(bf16), g)
            gqkv[:, cols] = join_windows(parts[0], parts[1], count).astype(bf16)
        gq[...] = jnp.zeros_like(gq)
        for s in range(2):
            low = pl.multiple_of(place[2 + s], SLACK)
            gq[pl.ds(low, KEYS + SLACK), :] += pltpu.roll(gkv[s], place[4 + s], 0)
        gqkv[:, inner:] = gq[:count].astype(bf16)
        gsum[...] += dot(gqkv[...], weight[:, : 3 * inner], NT)
        return carry

    lax.fori_loop(0, buf.shape[0], step, 0)
    unit, scale = norm_parts(start[...].astype(f32))
    grad = grad_after[...] + norm_back(unit, scale, gsum[...], gain[...].astype(f32))
    idx = index[...]
    grad_tok[...] = jnp.where(idx >= 0, 0.0, grad).astype(bf16)
    lanes = lax.broadcasted_iota(jnp.int32, (count, grad_prm.shape[0]), 1)
    onehot = (idx == lanes).astype(f32).astype(bf16)
    high = grad.astype(bf16)
    rest_one = grad - high.astype(f32)
    middle = rest_one.astype(bf16)
    low = (rest_one - middle.astype(f32)).astype(bf16)
    grad_prm[...] = dot(onehot, high, TN) + dot(onehot, middle, TN) + dot(onehot, low, TN)


vmem = pl.BlockSpec(memory_space=pltpu.VMEM)
smem = pl.BlockSpec(memory_space=pltpu.SMEM)
hbm = pl.BlockSpec(memory_space=pl.ANY)


def outside(arrays):
    return [pltpu.with_memory_space_constraint(a, pltpu.HBM) for a in arrays]


def shape(dims, kind):
    return jax.ShapeDtypeStruct(dims, kind)


def cost(flops, moved, exps=0):
    return pl.CostEstimate(flops=int(flops), bytes_accessed=int(moved), transcendentals=int(exps))


def move(value, target):
    pairs = []
    for i in range(32):
        z, y, x, c = target(i // 8, i // 4 % 2, i // 2 % 2, i % 2)
        pairs.append((i, ((z * 2 + y) * 2 + x) * 2 + c))
    return lax.ppermute(value, ("dp", "tp"), pairs)


def by_z(value, bits):
    return move(value, lambda z, y, x, c: (z ^ bits, y, x, c))


def by_x(value):
    return move(value, lambda z, y, x, c: (z, y, x ^ 1, c))


def by_y(value):
    return move(value, lambda z, y, x, c: (z, y ^ 1, x, c))


def by_xy(value):
    return move(value, lambda z, y, x, c: (z, y ^ 1, x ^ 1, c))


def split_yx(value):
    return move(value, lambda z, y, x, c: (z, y ^ 1, x, c) if c == 0 else (z, y, x ^ 1, c))


def across(value):
    axis = "tp"
    size = lax.axis_size(axis)
    return lax.ppermute(value, axis, [(i, i ^ 1) for i in range(size)])


def stack(pieces):
    return jnp.concatenate(pieces, 0)


def tie(value, *deps):
    return lax.optimization_barrier((value,) + deps)[0]


def by_core(even, odd):
    return jnp.where(lax.axis_index("tp") % 2 == 0, even, odd)


def places(rows):
    here = lax.axis_index("dp")
    slots = jnp.arange(8, dtype=jnp.int32)
    return (((here // 2) ^ (slots % 4)) * 2 + ((here % 2) ^ (slots // 4))) * rows


def column_plan(which, dy, block, lane, rows, sub=0, subs=1):
    return [(which, (j * subs + sub) * rows, rows, dy * 4 + j, block, lane) for j in range(4)]


def quad_plan(which, z, rows, dx, block, lane):
    return [(which, (dx + 2 * dy) * rows, rows, dy * 4 + z, block, lane) for dy in range(2)]


def on_device(
    tokens, prompt, qkv_weight, out_weight, up_weight, down_weight, gain_one, gain_two, segment_ids, pad_flags, cotangent
):
    dp, tp = lax.axis_size("dp"), lax.axis_size("tp")
    tok_dev, width = tokens.shape
    row_count, seq_len = segment_ids.shape
    count = tok_dev + HALO
    rows = qkv_weight.shape[0]
    inner = qkv_weight.shape[2]
    hidden = up_weight.shape[1]
    rank = lax.axis_index("tp")
    core = rank % 2
    row = rank // 2

    shard_a = jnp.concatenate([qkv_weight.reshape(rows, 3 * inner), out_weight.T], axis=1)
    shard_d = down_weight.T
    half = hidden // 2
    up_one, up_two = up_weight[:, :half], up_weight[:, half:]
    down_one, down_two = shard_d[:, :half], shard_d[:, half:]

    if dp == 8:
        a_one, a_two = by_z(shard_a, 1), by_z(shard_a, 2)
        d_x, d_y = by_x(down_two), by_y(down_two)
        a_three = by_z(a_two, 1)
        segment_ids, pad_flags = lax.optimization_barrier((segment_ids, pad_flags, a_two))[:2]
        prompt = tie(prompt, a_three)

    sent = (1 - core) * (tok_dev - HALO)
    both = stack(
        [
            lax.dynamic_slice_in_dim(tokens, sent, HALO, 0),
            lax.dynamic_slice_in_dim(cotangent, sent, HALO, 0),
        ]
    )
    both = across(both)
    main, side = HALO * core, tok_dev * (1 - core)

    first = core * (seq_len - count)
    seg = lax.dynamic_slice(segment_ids, (row, first), (1, count))
    pad = lax.dynamic_slice(pad_flags, (row, first), (1, count))
    position = jnp.arange(count, dtype=jnp.int32)[None, :]
    live = pad == 0
    index = jnp.full((1, count), -1, jnp.int32)
    begins, keys = [], []
    for s in range(2):
        own = live & (seg == 2 * core + s)
        begin = jnp.min(jnp.where(own, position, count))
        offset = position - begin
        index = jnp.where(own & (offset >= 1) & (offset <= PROMPTS), offset - 1, index)
        begins.append(jnp.minimum(begin, count - KEYS))
        keys.append(lax.dynamic_slice(jnp.where(own, seg, -1), (0, begins[s]), (1, KEYS)))
    column = lambda r: r.reshape(r.shape[1], 1)
    index_col = column(index)
    lows = [b // SLACK * SLACK for b in begins]
    shifts = [b - a for a, b in zip(lows, begins)]
    back_shifts = [(KEYS + SLACK - b) % (KEYS + SLACK) for b in shifts]
    place = jnp.stack([main, side] + lows + shifts + back_shifts).astype(jnp.int32)

    gain_one, gain_two = gain_one[None, :], gain_two[None, :]
    limit = lambda mib: pltpu.CompilerParams(vmem_limit_bytes=mib << 20)
    act = count * width
    mac = 2 * act * width
    start, normed, cot = pl.pallas_call(
        enter_kernel,
        name="enter",
        in_specs=[smem] + [vmem] * 7,
        out_specs=[vmem] * 3,
        out_shape=[pltpu.HBM((count, width), bf16)] * 3,
        cost_estimate=cost(2 * act * 64, 10 * act),
        compiler_params=limit(12),
    )(place, tokens, both[:HALO], cotangent, both[HALO:], prompt, index_col, gain_one)

    blocks = tp
    heads = width // HD
    dma = pltpu.SemaphoreType.DMA
    pair_flops = 2 * 2 * WIN * KEYS * HD * heads

    def attend(plan, arrays):
        return pl.pallas_call(
            functools.partial(attend_kernel, plan),
            name="attend",
            in_specs=[smem] * 2 + [hbm] * 2 + [vmem] * 4 + [hbm] * len(arrays),
            out_specs=[hbm, vmem, hbm, hbm],
            out_shape=[
                pltpu.HBM((count, width), f32),
                shape((count, width), bf16),
                pltpu.HBM((blocks, count, inner), bf16),
                pltpu.HBM((blocks, 2, KEYS, 2 * inner), bf16),
            ],
            scratch_shapes=[
                pltpu.VMEM((blocks, width, width), bf16),
                pltpu.VMEM((2, WIN, KEYS), f32),
                pltpu.VMEM((count, inner), bf16),
                pltpu.VMEM((count + SLACK, 2 * inner), f32),
                pltpu.VMEM((count, width), bf16),
                pltpu.VMEM((count, width), bf16),
                pltpu.VMEM((count, width), f32),
                pltpu.VMEM((blocks, count, inner), bf16),
                pltpu.VMEM((blocks, 2, KEYS, 2 * inner), bf16),
                dma((blocks,)),
                dma((4,)),
            ],
            cost_estimate=cost(4 * mac + 2 * pair_flops, 8 * width * width + 16 * act, 2 * WIN * KEYS * heads),
            compiler_params=limit(24),
        )(place, table, *outside([normed, start]), gain_two, column(seg), *keys, *outside(arrays))

    def mlp(plans, arrays, held, size, last):
        outs = [pltpu.HBM((count, width), f32)] * 2
        if last:
            outs = [shape((count, width), bf16), shape((count, width), f32), shape((count, width), bf16)]
        return pl.pallas_call(
            functools.partial(mlp_kernel, plans, last),
            name="mlp_last" if last else "mlp",
            in_specs=[smem] + [vmem] * 2 + [hbm] * (len(held) + len(arrays)),
            out_specs=[vmem if last else hbm] * len(outs),
            out_shape=outs,
            scratch_shapes=[pltpu.VMEM((count, width), kind) for kind in (bf16, f32, f32, f32)]
            + [pltpu.VMEM((size, width, width), bf16)] * 2
            + [dma((2, size)), dma((len(held),))],
            cost_estimate=cost(4 * size * mac, 4 * size * width * width + 20 * act, 2 * size * act),
            compiler_params=limit(40 if last else 24),
        )(table, normed_two, gain_two, *outside(held), *outside(arrays))

    if dp == 8:
        table = places(rows)
        m_own = stack([up_one, down_one, up_two])
        a_col = stack([shard_a, a_one, a_two, a_three])
        a_col, m_own, d_x, d_y, both, index_col, place, *keys = lax.optimization_barrier(
            (a_col, m_own, d_x, d_y, both, index_col, place, *keys)
        )
        a_x, a_y = by_x(a_col), by_y(a_col)
        m_one, m_two = by_z(m_own, 1), by_z(m_own, 2)
        d_diag = split_yx(tie(by_core(d_x, d_y), a_x))
        a_diag = split_yx(tie(by_core(a_x, a_y), m_one, normed))
        m_three = by_z(m_two, 1)
        a_pairs = [(v, across(v)) for v in (a_col, a_x, a_y, a_diag)]
        arrays_a, plan_a = [], []
        for which, pair in enumerate(a_pairs):
            for dc, array in enumerate(pair):
                plan_a += column_plan(len(arrays_a), which // 2, (which % 2) * 2 + dc, 0, rows)
                arrays_a.append(array)
        m_col = tie(stack([m_own, m_one, m_two, m_three]), a_diag)
        d_quad = tie(stack([down_two, d_x, d_y, d_diag]), a_diag)
        m_x, m_y = by_x(m_col), by_y(m_col)
        d_one, d_two = by_z(d_quad, 1), by_z(d_quad, 2)
        arrays_a[0] = tie(arrays_a[0], m_col, d_quad)
        after, normed_two, q_all, kv_all = attend(plan_a, arrays_a)
        m_x, m_y, d_one, d_two, normed_two = lax.optimization_barrier((m_x, m_y, d_one, d_two, normed_two))
        m_diag = split_yx(by_core(m_x, m_y))
        d_three = by_z(d_two, 1)
        def plan(dx, second, block):
            near = [4 * dx + k for k in range(4)]
            ups = [e for k in range(4) for e in column_plan(near[k], k // 2, block, (k % 2) * half, rows, 2 * second, 3)]
            if second:
                downs = [e for k in range(8) for e in quad_plan(8 + k, k // 2, rows, dx, block, (k % 2) * half)]
            else:
                downs = [e for k in range(4) for e in column_plan(near[k], k // 2, block, (k % 2) * half, rows, 1, 3)]
            return ups, downs

        near = [m_col, across(m_col), m_y, across(m_y)]
        early = [v for k in (d_quad, d_one, d_two) for v in (k, across(k))]
        near[2], *early = lax.optimization_barrier((near[2], *early))
        total, gsum = mlp(plan(0, 0, 0), near, [cot, after], 1, False)
        m_diag, d_three = lax.optimization_barrier((m_diag, d_three, gsum))[:2]
        far = [m_x, across(m_x), m_diag, across(m_diag)] + early + [d_three, across(d_three)]
        plans = [sum(kind, []) for kind in zip(*(plan(*k) for k in ((0, 1, 0), (1, 0, 1), (1, 1, 2))))]
        output, grad_after, branch = mlp(plans, near + far, [cot, after, total, gsum], 3, True)
    else:
        table = jnp.zeros((8,), jnp.int32)

        def whole(shard):
            return lax.all_gather(lax.all_gather(shard, "dp", axis=0, tiled=True), "tp", axis=0, tiled=True)

        arrays_a, plan_a = [whole(shard_a)], [(0, t * width, width, 0, t, 0) for t in range(tp)]
        after, normed_two, q_all, kv_all = attend(plan_a, arrays_a)
        pairs = [whole(up_one), whole(down_one), whole(up_two), whole(down_two)]

        def plan(k, block, kind):
            which = k // 2 * 2 + kind
            return [(which, (k % 2 * 2 + dc) * width, width, 0, block, dc * half) for dc in range(2)]

        total, gsum = mlp([plan(0, 0, kind) for kind in range(2)], pairs[:2], [cot, after], 1, False)
        plans = [[e for k in (1, 2, 3) for e in plan(k, k - 1, kind)] for kind in range(2)]
        output, grad_after, branch = mlp(plans, pairs, [cot, after, total, gsum], 3, True)

    grad_tok, grad_prm = pl.pallas_call(
        functools.partial(back_kernel, plan_a),
        name="back",
        in_specs=[smem] * 2 + [vmem] * 10 + [hbm] * len(arrays_a),
        out_specs=[vmem] * 2,
        out_shape=[shape((count, width), bf16), shape((64, width), f32)],
        scratch_shapes=[
            pltpu.VMEM((blocks, width, width), bf16),
            pltpu.VMEM((2, KEYS, WIN), f32),
            pltpu.VMEM((count, inner), bf16),
            pltpu.VMEM((count + SLACK, 2 * inner), f32),
            pltpu.VMEM((2, KEYS + SLACK, 2 * inner), f32),
            pltpu.VMEM((count, 3 * inner), bf16),
            pltpu.VMEM((count, width), f32),
            dma((blocks,)),
        ],
        cost_estimate=cost(4 * mac + 5 * pair_flops, 8 * width * width + 16 * act, 2 * WIN * KEYS * heads),
        compiler_params=limit(32),
    )(
        place, table, branch, grad_after, start, q_all, kv_all, gain_one, seg, column(keys[0]), column(keys[1]), index_col,
        *outside(arrays_a),
    )

    mine = lax.dynamic_slice_in_dim(column(seg), main + sent, HALO, 0) // 2 == core

    def settle(window):
        theirs = across(lax.dynamic_slice_in_dim(window, side, HALO, 0))
        own = lax.dynamic_slice_in_dim(window, main, tok_dev, 0)
        kept = lax.dynamic_slice_in_dim(own, sent, HALO, 0)
        return lax.dynamic_update_slice_in_dim(own, jnp.where(mine, kept, theirs), sent, 0)

    prm = grad_prm[:PROMPTS]
    if dp == 8:
        mid = width // 2
        lanes = lambda k: lax.dynamic_slice(prm, (0, k * mid), (PROMPTS, mid)).astype(bf16)
        part = lanes(core).astype(f32) + across(lanes(1 - core)).astype(f32)
        for turns in ((by_x, by_y, by_xy), tuple(functools.partial(by_z, bits=k) for k in (1, 2, 3))):
            sent_prm = part.astype(bf16)
            one, two, three = (turn(sent_prm).astype(f32) for turn in turns)
            part = (sent_prm.astype(f32) + one) + (two + three)
        part = (part / (row_count * dp)).astype(bf16)
        other = across(part)
        grad_prm = jnp.where(core == 0, jnp.concatenate([part, other], 1), jnp.concatenate([other, part], 1))
    else:
        grad_prm = (lax.psum(prm, ("dp", "tp")) / (row_count * dp)).astype(bf16)
    return (settle(output), settle(grad_tok), grad_prm)


def solution(mesh):
    return jax.shard_map(
        on_device,
        mesh=mesh,
        in_specs=(
            P(("dp", "tp"), None),
            P(),
            P("dp", None, "tp"),
            P("tp", "dp"),
            P("dp", "tp"),
            P("tp", "dp"),
            P(),
            P(),
            P("dp", None),
            P("dp", None),
            P(("dp", "tp"), None),
        ),
        out_specs=(P(("dp", "tp"), None), P(("dp", "tp"), None), P()),
        check_vma=False,
    )
```

```python
import functools

import jax
import jax.numpy as jnp
from jax import lax
from jax.experimental import pallas as pl
from jax.experimental.pallas import tpu as pltpu
from jax.sharding import PartitionSpec as P

HD = 64
PROMPTS = 50
HALO = 32
WIN = 304
KEYS = 256
SLACK = 8
NT = (((1,), (1,)), ((), ()))
NN = (((1,), (0,)), ((), ()))
TN = (((0,), (0,)), ((), ()))
eps = 1e-6
fill = -1e30
floor = -1e29
bf16 = jnp.bfloat16
f32 = jnp.float32


def dot(a, b, dims=NN):
    return lax.dot_general(a, b, dims, preferred_element_type=f32)


def norm_parts(values):
    centred = values - jnp.mean(values, axis=-1, keepdims=True)
    scale = lax.rsqrt(jnp.mean(centred * centred, axis=-1, keepdims=True) + eps)
    return centred * scale, scale


def norm_back(unit, scale, grad, gain):
    u = grad * gain
    return scale * (
        u - jnp.mean(u, axis=-1, keepdims=True) - unit * jnp.mean(u * unit, axis=-1, keepdims=True)
    )


def window_starts(count):
    return (0, count - WIN)


def join_windows(first, second, count):
    low = count - WIN
    return jnp.concatenate([first[:low], first[low:] + second[: WIN - low], second[WIN - low :]], 0)


def fetch(plan, table, refs, buf, sems, later=False):
    for which, source, rows, slot, block, lane in plan:
        if (block > 0) != later:
            continue
        lanes = refs[which].shape[1]
        pltpu.make_async_copy(
            refs[which].at[pl.ds(source, rows)],
            buf.at[block, pl.ds(pl.multiple_of(table[slot], 16), rows), pl.ds(lane, lanes)],
            sems.at[block],
        ).start()


def arrive(buf, sems, block):
    pltpu.make_async_copy(buf.at[block], buf.at[block], sems.at[block]).wait()


def shifted_in(wide, place, s):
    low = pl.multiple_of(place[2 + s], SLACK)
    value = wide[pl.ds(low, KEYS + SLACK), :]
    return pltpu.roll(value, place[6 + s], 0)[:KEYS]


def enter_kernel(place, own, own_halo, cot, cot_halo, prompt, index, gain, start, normed, cot_out):
    main = pl.multiple_of(place[0], HALO)
    side = pl.multiple_of(place[1], HALO)
    rows = own.shape[0]
    start[pl.ds(main, rows), :] = own[...]
    start[pl.ds(side, HALO), :] = own_halo[...]
    cot_out[pl.ds(main, rows), :] = cot[...]
    cot_out[pl.ds(side, HALO), :] = cot_halo[...]
    idx = index[...]
    lanes = lax.broadcasted_iota(jnp.int32, (idx.shape[0], PROMPTS), 1)
    onehot = (idx == lanes).astype(f32).astype(bf16)
    picked = dot(onehot, prompt[...])
    value = jnp.where(idx >= 0, picked, start[...].astype(f32))
    start[...] = value.astype(bf16)
    unit, _ = norm_parts(value)
    normed[...] = (unit * gain[...].astype(f32)).astype(bf16)


def attend_kernel(plan, place, table, normed, start, gain, qseg, krow_a, krow_b, *rest):
    n = len(rest) - 15
    refs, rest = rest[:n], rest[n:]
    after_out, normed_two, q_out, kv_out, buf, bias, mix, wide, normed_in, start_in, *rest = rest
    after, q_kept, kv_kept, sems, own_sems = rest
    count = normed.shape[0]
    inner = q_out.shape[2]
    heads = inner // HD
    own = [
        pltpu.make_async_copy(normed, normed_in, own_sems.at[0]),
        pltpu.make_async_copy(start, start_in, own_sems.at[1]),
    ]
    own[0].start()
    fetch(plan, table, refs, buf, sems)
    own[1].start()
    starts = window_starts(count)
    for s, krow in enumerate((krow_a, krow_b)):
        bias[s] = jnp.where(qseg[starts[s] : starts[s] + WIN, :] == krow[...], 0.0, fill)
    wide[count:] = jnp.zeros_like(wide[count:])
    for copy in own:
        copy.wait()
    after[...] = start_in[...].astype(f32)
    arrive(buf, sems, 0)
    fetch(plan, table, refs, buf, sems, later=True)

    def step(block, carry):
        @pl.when(block > 0)
        def _():
            arrive(buf, sems, block)

        weight = buf.at[block]
        both = dot(normed_in[...], weight[:, : 3 * inner])
        q_all = both[:, :inner].astype(bf16) * bf16(HD**-0.5)
        q_kept[block] = q_all
        wide[:count] = both[:, inner:]
        pairs = [shifted_in(wide, place, s).astype(bf16) for s in range(2)]
        for s in range(2):
            kv_kept[block, s] = pairs[s]
        pltpu.make_async_copy(q_kept.at[block], q_out.at[block], own_sems.at[2]).start()
        pltpu.make_async_copy(kv_kept.at[block], kv_out.at[block], own_sems.at[3]).start()
        for h in range(heads):
            parts = []
            for s in range(2):
                q = q_all[starts[s] : starts[s] + WIN, h * HD : (h + 1) * HD]
                k = pairs[s][:, h * HD : (h + 1) * HD]
                v = pairs[s][:, inner + h * HD : inner + (h + 1) * HD]
                scores = dot(q, k, NT) + bias[s]
                top = jnp.maximum(jnp.max(scores, axis=-1, keepdims=True), floor)
                weights = jnp.exp(scores - top)
                total = jnp.maximum(jnp.sum(weights, axis=-1, keepdims=True), 1e-30)
                probs = (weights * (1.0 / total)).astype(bf16)
                parts.append(dot(probs, v))
            mix[:, h * HD : (h + 1) * HD] = join_windows(parts[0], parts[1], count).astype(bf16)
        after[...] += dot(mix[...], weight[:, 3 * inner :], NT)
        return carry

    lax.fori_loop(0, buf.shape[0], step, 0)
    give = pltpu.make_async_copy(after, after_out, own_sems.at[0])
    give.start()
    unit, _ = norm_parts(after[...])
    normed_two[...] = (unit * gain[...].astype(f32)).astype(bf16)
    give.wait()
    pltpu.make_async_copy(q_kept, q_out, own_sems.at[2]).wait()
    pltpu.make_async_copy(kv_kept, kv_out, own_sems.at[3]).wait()


def mlp_kernel(plans, last, table, normed_two, gain, *rest):
    n = len(rest) - (15 if last else 12)
    held, refs, rest = rest[: 4 if last else 2], rest[4 if last else 2 :][:n], rest[4 if last else 2 :][n:]
    if last:
        output, grad_after, branch, cot, after, total, gsum, up, down, sems, own_sems = rest
    else:
        total_out, gsum_out, cot, after, total, gsum, up, down, sems, own_sems = rest
    fetch(plans[0], table, refs, up, sems.at[0])
    fetch(plans[1], table, refs, down, sems.at[1])
    own = [
        pltpu.make_async_copy(source, place, own_sems.at[k])
        for k, (source, place) in enumerate(zip(held, (cot, after, total, gsum)))
    ]
    for copy in own:
        copy.start()
    fetch(plans[0], table, refs, up, sems.at[0], later=True)
    fetch(plans[1], table, refs, down, sems.at[1], later=True)

    def step(block, carry):
        arrive(up, sems.at[0], block)
        pre = dot(normed_two[...], up[block])
        cdf = 0.5 + 0.5 * lax.erf(pre * (0.5**0.5))
        slope = cdf + pre * (jnp.exp(-0.5 * pre * pre) * 0.3989422804014327)
        act = (pre * cdf).astype(bf16)
        arrive(down, sems.at[1], block)
        if isinstance(block, int):
            own[0].wait()
        back = dot(cot[...], down[block])
        grad_pre = (back * slope).astype(bf16)
        if last:
            if isinstance(block, int):
                own[2].wait()
                own[3].wait()
            total[...] += dot(act, down[block], NT)
            gsum[...] += dot(grad_pre, up[block], NT)
        else:
            own[1].wait()
            total[...] = after[...] + dot(act, down[block], NT)
            give = pltpu.make_async_copy(total, total_out, own_sems.at[0])
            give.start()
            gsum[...] = dot(grad_pre, up[block], NT)
            give_more = pltpu.make_async_copy(gsum, gsum_out, own_sems.at[1])
            give_more.start()
            give.wait()
            give_more.wait()
        return carry

    step(0, 0)
    if last:
        lax.fori_loop(1, up.shape[0], step, 0)
        own[1].wait()
        output[...] = total[...].astype(bf16)
        unit, scale = norm_parts(after[...])
        grad = cot[...].astype(f32) + norm_back(unit, scale, gsum[...], gain[...].astype(f32))
        grad_after[...] = grad
        branch[...] = grad.astype(bf16)


def back_kernel(plan, place, table, branch, grad_after, start, q_all, kv_all, gain, qrow, kcol_a, kcol_b, index, *rest):
    n = len(rest) - 10
    refs, (grad_tok, grad_prm, buf, bias, gmix, gq, gkv, gqkv, gsum, sems) = rest[:n], rest[n:]
    count = branch.shape[0]
    inner = q_all.shape[2]
    heads = inner // HD
    fetch(plan, table, refs, buf, sems)
    starts = window_starts(count)
    for s, kcol in enumerate((kcol_a, kcol_b)):
        bias[s] = jnp.where(kcol[...] == qrow[...][:, starts[s] : starts[s] + WIN], 0.0, fill)
    gsum[...] = jnp.zeros_like(gsum)
    gkv[...] = jnp.zeros_like(gkv)
    arrive(buf, sems, 0)
    fetch(plan, table, refs, buf, sems, later=True)

    def step(block, carry):
        @pl.when(block > 0)
        def _():
            arrive(buf, sems, block)

        weight = buf.at[block]
        gmix[...] = dot(branch[...], weight[:, 3 * inner :]).astype(bf16)
        for h in range(heads):
            cols = slice(h * HD, (h + 1) * HD)
            late = slice(inner + h * HD, inner + (h + 1) * HD)
            parts = []
            for s in range(2):
                rows = slice(starts[s], starts[s] + WIN)
                q = q_all[block, rows, cols]
                k = kv_all[block, s, :, cols]
                v = kv_all[block, s, :, late]
                g = gmix[rows, cols]
                scores = dot(k, q, NT) + bias[s]
                top = jnp.maximum(jnp.max(scores, axis=0, keepdims=True), floor)
                weights = jnp.exp(scores - top)
                total = jnp.maximum(jnp.sum(weights, axis=0, keepdims=True), 1e-30)
                probs = weights * (1.0 / total)
                grad_probs = dot(v, g, NT)
                centre = jnp.sum(grad_probs * probs, axis=0, keepdims=True)
                grad_scores = (probs * (grad_probs - centre)).astype(bf16)
                parts.append(dot(grad_scores, k * bf16(HD**-0.5), TN))
                gkv[s, :KEYS, cols] = dot(grad_scores, q)
                gkv[s, :KEYS, late] = dot(probs.astype(bf16), g)
            gqkv[:, cols] = join_windows(parts[0], parts[1], count).astype(bf16)
        gq[...] = jnp.zeros_like(gq)
        for s in range(2):
            low = pl.multiple_of(place[2 + s], SLACK)
            gq[pl.ds(low, KEYS + SLACK), :] += pltpu.roll(gkv[s], place[4 + s], 0)
        gqkv[:, inner:] = gq[:count].astype(bf16)
        gsum[...] += dot(gqkv[...], weight[:, : 3 * inner], NT)
        return carry

    lax.fori_loop(0, buf.shape[0], step, 0)
    unit, scale = norm_parts(start[...].astype(f32))
    grad = grad_after[...] + norm_back(unit, scale, gsum[...], gain[...].astype(f32))
    idx = index[...]
    grad_tok[...] = jnp.where(idx >= 0, 0.0, grad).astype(bf16)
    lanes = lax.broadcasted_iota(jnp.int32, (count, grad_prm.shape[0]), 1)
    onehot = (idx == lanes).astype(f32).astype(bf16)
    high = grad.astype(bf16)
    rest_one = grad - high.astype(f32)
    middle = rest_one.astype(bf16)
    low = (rest_one - middle.astype(f32)).astype(bf16)
    grad_prm[...] = dot(onehot, high, TN) + dot(onehot, middle, TN) + dot(onehot, low, TN)


vmem = pl.BlockSpec(memory_space=pltpu.VMEM)
smem = pl.BlockSpec(memory_space=pltpu.SMEM)
hbm = pl.BlockSpec(memory_space=pl.ANY)


def outside(arrays):
    return [pltpu.with_memory_space_constraint(a, pltpu.HBM) for a in arrays]


def shape(dims, kind):
    return jax.ShapeDtypeStruct(dims, kind)


def cost(flops, moved, exps=0):
    return pl.CostEstimate(flops=int(flops), bytes_accessed=int(moved), transcendentals=int(exps))


def move(value, target):
    pairs = []
    for i in range(32):
        z, y, x, c = target(i // 8, i // 4 % 2, i // 2 % 2, i % 2)
        pairs.append((i, ((z * 2 + y) * 2 + x) * 2 + c))
    return lax.ppermute(value, ("dp", "tp"), pairs)


def by_z(value, bits):
    return move(value, lambda z, y, x, c: (z ^ bits, y, x, c))


def by_x(value):
    return move(value, lambda z, y, x, c: (z, y, x ^ 1, c))


def by_y(value):
    return move(value, lambda z, y, x, c: (z, y ^ 1, x, c))


def by_xy(value):
    return move(value, lambda z, y, x, c: (z, y ^ 1, x ^ 1, c))


def split_yx(value):
    return move(value, lambda z, y, x, c: (z, y ^ 1, x, c) if c == 0 else (z, y, x ^ 1, c))


def across(value):
    axis = "tp"
    size = lax.axis_size(axis)
    return lax.ppermute(value, axis, [(i, i ^ 1) for i in range(size)])


def stack(pieces):
    return jnp.concatenate(pieces, 0)


def tie(value, *deps):
    return lax.optimization_barrier((value,) + deps)[0]


def by_core(even, odd):
    return jnp.where(lax.axis_index("tp") % 2 == 0, even, odd)


def places(rows):
    here = lax.axis_index("dp")
    slots = jnp.arange(8, dtype=jnp.int32)
    return (((here // 2) ^ (slots % 4)) * 2 + ((here % 2) ^ (slots // 4))) * rows


def column_plan(which, dy, block, lane, rows, sub=0, subs=1):
    return [(which, (j * subs + sub) * rows, rows, dy * 4 + j, block, lane) for j in range(4)]


def quad_plan(which, z, rows, dx, block, lane):
    return [(which, (dx + 2 * dy) * rows, rows, dy * 4 + z, block, lane) for dy in range(2)]


def on_device(
    tokens, prompt, qkv_weight, out_weight, up_weight, down_weight, gain_one, gain_two, segment_ids, pad_flags, cotangent
):
    dp, tp = lax.axis_size("dp"), lax.axis_size("tp")
    tok_dev, width = tokens.shape
    row_count, seq_len = segment_ids.shape
    count = tok_dev + HALO
    rows = qkv_weight.shape[0]
    inner = qkv_weight.shape[2]
    hidden = up_weight.shape[1]
    rank = lax.axis_index("tp")
    core = rank % 2
    row = rank // 2

    shard_a = jnp.concatenate([qkv_weight.reshape(rows, 3 * inner), out_weight.T], axis=1)
    shard_d = down_weight.T
    half = hidden // 2
    up_one, up_two = up_weight[:, :half], up_weight[:, half:]
    down_one, down_two = shard_d[:, :half], shard_d[:, half:]

    if dp == 8:
        a_one, a_two = by_z(shard_a, 1), by_z(shard_a, 2)
        d_x, d_y = by_x(down_two), by_y(down_two)
        a_three = by_z(a_two, 1)
        segment_ids, pad_flags = lax.optimization_barrier((segment_ids, pad_flags, a_two))[:2]
        prompt = tie(prompt, a_three)

    sent = (1 - core) * (tok_dev - HALO)
    both = stack(
        [
            lax.dynamic_slice_in_dim(tokens, sent, HALO, 0),
            lax.dynamic_slice_in_dim(cotangent, sent, HALO, 0),
        ]
    )
    both = across(both)
    main, side = HALO * core, tok_dev * (1 - core)

    first = core * (seq_len - count)
    seg = lax.dynamic_slice(segment_ids, (row, first), (1, count))
    pad = lax.dynamic_slice(pad_flags, (row, first), (1, count))
    position = jnp.arange(count, dtype=jnp.int32)[None, :]
    live = pad == 0
    index = jnp.full((1, count), -1, jnp.int32)
    begins, keys = [], []
    for s in range(2):
        own = live & (seg == 2 * core + s)
        begin = jnp.min(jnp.where(own, position, count))
        offset = position - begin
        index = jnp.where(own & (offset >= 1) & (offset <= PROMPTS), offset - 1, index)
        begins.append(jnp.minimum(begin, count - KEYS))
        keys.append(lax.dynamic_slice(jnp.where(own, seg, -1), (0, begins[s]), (1, KEYS)))
    column = lambda r: r.reshape(r.shape[1], 1)
    index_col = column(index)
    lows = [b // SLACK * SLACK for b in begins]
    shifts = [b - a for a, b in zip(lows, begins)]
    back_shifts = [(KEYS + SLACK - b) % (KEYS + SLACK) for b in shifts]
    place = jnp.stack([main, side] + lows + shifts + back_shifts).astype(jnp.int32)

    gain_one, gain_two = gain_one[None, :], gain_two[None, :]
    limit = lambda mib: pltpu.CompilerParams(vmem_limit_bytes=mib << 20)
    act = count * width
    mac = 2 * act * width
    start, normed, cot = pl.pallas_call(
        enter_kernel,
        name="enter",
        in_specs=[smem] + [vmem] * 7,
        out_specs=[vmem] * 3,
        out_shape=[pltpu.HBM((count, width), bf16)] * 3,
        cost_estimate=cost(2 * act * 64, 10 * act),
        compiler_params=limit(12),
    )(place, tokens, both[:HALO], cotangent, both[HALO:], prompt, index_col, gain_one)

    blocks = tp
    heads = width // HD
    dma = pltpu.SemaphoreType.DMA
    pair_flops = 2 * 2 * WIN * KEYS * HD * heads

    def attend(plan, arrays):
        return pl.pallas_call(
            functools.partial(attend_kernel, plan),
            name="attend",
            in_specs=[smem] * 2 + [hbm] * 2 + [vmem] * 4 + [hbm] * len(arrays),
            out_specs=[hbm, vmem, hbm, hbm],
            out_shape=[
                pltpu.HBM((count, width), f32),
                shape((count, width), bf16),
                pltpu.HBM((blocks, count, inner), bf16),
                pltpu.HBM((blocks, 2, KEYS, 2 * inner), bf16),
            ],
            scratch_shapes=[
                pltpu.VMEM((blocks, width, width), bf16),
                pltpu.VMEM((2, WIN, KEYS), f32),
                pltpu.VMEM((count, inner), bf16),
                pltpu.VMEM((count + SLACK, 2 * inner), f32),
                pltpu.VMEM((count, width), bf16),
                pltpu.VMEM((count, width), bf16),
                pltpu.VMEM((count, width), f32),
                pltpu.VMEM((blocks, count, inner), bf16),
                pltpu.VMEM((blocks, 2, KEYS, 2 * inner), bf16),
                dma((blocks,)),
                dma((4,)),
            ],
            cost_estimate=cost(4 * mac + 2 * pair_flops, 8 * width * width + 16 * act, 2 * WIN * KEYS * heads),
            compiler_params=limit(24),
        )(place, table, *outside([normed, start]), gain_two, column(seg), *keys, *outside(arrays))

    def mlp(plans, arrays, held, size, last):
        outs = [pltpu.HBM((count, width), f32)] * 2
        if last:
            outs = [shape((count, width), bf16), shape((count, width), f32), shape((count, width), bf16)]
        return pl.pallas_call(
            functools.partial(mlp_kernel, plans, last),
            name="mlp_last" if last else "mlp",
            in_specs=[smem] + [vmem] * 2 + [hbm] * (len(held) + len(arrays)),
            out_specs=[vmem if last else hbm] * len(outs),
            out_shape=outs,
            scratch_shapes=[pltpu.VMEM((count, width), kind) for kind in (bf16, f32, f32, f32)]
            + [pltpu.VMEM((size, width, width), bf16)] * 2
            + [dma((2, size)), dma((len(held),))],
            cost_estimate=cost(4 * size * mac, 4 * size * width * width + 20 * act, 2 * size * act),
            compiler_params=limit(40 if last else 24),
        )(table, normed_two, gain_two, *outside(held), *outside(arrays))

    if dp == 8:
        table = places(rows)
        m_own = stack([up_one, down_one, up_two])
        a_col = stack([shard_a, a_one, a_two, a_three])
        a_col, m_own, d_x, d_y, both, index_col, place, *keys = lax.optimization_barrier(
            (a_col, m_own, d_x, d_y, both, index_col, place, *keys)
        )
        a_x, a_y = by_x(a_col), by_y(a_col)
        m_one, m_two = by_z(m_own, 1), by_z(m_own, 2)
        d_diag = split_yx(tie(by_core(d_x, d_y), a_x))
        a_diag = split_yx(tie(by_core(a_x, a_y), m_one, normed))
        m_three = by_z(m_two, 1)
        a_pairs = [(v, across(v)) for v in (a_col, a_x, a_y, a_diag)]
        arrays_a, plan_a = [], []
        for which, pair in enumerate(a_pairs):
            for dc, array in enumerate(pair):
                plan_a += column_plan(len(arrays_a), which // 2, (which % 2) * 2 + dc, 0, rows)
                arrays_a.append(array)
        m_col = tie(stack([m_own, m_one, m_two, m_three]), a_diag)
        d_quad = tie(stack([down_two, d_x, d_y, d_diag]), a_diag)
        m_x, m_y = by_x(m_col), by_y(m_col)
        d_one, d_two = by_z(d_quad, 1), by_z(d_quad, 2)
        arrays_a[0] = tie(arrays_a[0], m_col, d_quad)
        after, normed_two, q_all, kv_all = attend(plan_a, arrays_a)
        m_x, m_y, d_one, d_two, normed_two = lax.optimization_barrier((m_x, m_y, d_one, d_two, normed_two))
        m_diag = split_yx(by_core(m_x, m_y))
        d_three = by_z(d_two, 1)
        def plan(dx, second, block):
            near = [4 * dx + k for k in range(4)]
            ups = [e for k in range(4) for e in column_plan(near[k], k // 2, block, (k % 2) * half, rows, 2 * second, 3)]
            if second:
                downs = [e for k in range(8) for e in quad_plan(8 + k, k // 2, rows, dx, block, (k % 2) * half)]
            else:
                downs = [e for k in range(4) for e in column_plan(near[k], k // 2, block, (k % 2) * half, rows, 1, 3)]
            return ups, downs

        near = [m_col, across(m_col), m_y, across(m_y)]
        early = [v for k in (d_quad, d_one, d_two) for v in (k, across(k))]
        near[2], *early = lax.optimization_barrier((near[2], *early))
        total, gsum = mlp(plan(0, 0, 0), near, [cot, after], 1, False)
        m_diag, d_three = lax.optimization_barrier((m_diag, d_three, gsum))[:2]
        far = [m_x, across(m_x), m_diag, across(m_diag)] + early + [d_three, across(d_three)]
        plans = [sum(kind, []) for kind in zip(*(plan(*k) for k in ((0, 1, 0), (1, 0, 1), (1, 1, 2))))]
        output, grad_after, branch = mlp(plans, near + far, [cot, after, total, gsum], 3, True)
    else:
        table = jnp.zeros((8,), jnp.int32)

        def whole(shard):
            return lax.all_gather(lax.all_gather(shard, "dp", axis=0, tiled=True), "tp", axis=0, tiled=True)

        arrays_a, plan_a = [whole(shard_a)], [(0, t * width, width, 0, t, 0) for t in range(tp)]
        after, normed_two, q_all, kv_all = attend(plan_a, arrays_a)
        pairs = [whole(up_one), whole(down_one), whole(up_two), whole(down_two)]

        def plan(k, block, kind):
            which = k // 2 * 2 + kind
            return [(which, (k % 2 * 2 + dc) * width, width, 0, block, dc * half) for dc in range(2)]

        total, gsum = mlp([plan(0, 0, kind) for kind in range(2)], pairs[:2], [cot, after], 1, False)
        plans = [[e for k in (1, 2, 3) for e in plan(k, k - 1, kind)] for kind in range(2)]
        output, grad_after, branch = mlp(plans, pairs, [cot, after, total, gsum], 3, True)

    grad_tok, grad_prm = pl.pallas_call(
        functools.partial(back_kernel, plan_a),
        name="back",
        in_specs=[smem] * 2 + [vmem] * 10 + [hbm] * len(arrays_a),
        out_specs=[vmem] * 2,
        out_shape=[shape((count, width), bf16), shape((64, width), f32)],
        scratch_shapes=[
            pltpu.VMEM((blocks, width, width), bf16),
            pltpu.VMEM((2, KEYS, WIN), f32),
            pltpu.VMEM((count, inner), bf16),
            pltpu.VMEM((count + SLACK, 2 * inner), f32),
            pltpu.VMEM((2, KEYS + SLACK, 2 * inner), f32),
            pltpu.VMEM((count, 3 * inner), bf16),
            pltpu.VMEM((count, width), f32),
            dma((blocks,)),
        ],
        cost_estimate=cost(4 * mac + 5 * pair_flops, 8 * width * width + 16 * act, 2 * WIN * KEYS * heads),
        compiler_params=limit(32),
    )(
        place, table, branch, grad_after, start, q_all, kv_all, gain_one, seg, column(keys[0]), column(keys[1]), index_col,
        *outside(arrays_a),
    )

    mine = lax.dynamic_slice_in_dim(column(seg), main + sent, HALO, 0) // 2 == core

    def settle(window):
        theirs = across(lax.dynamic_slice_in_dim(window, side, HALO, 0))
        own = lax.dynamic_slice_in_dim(window, main, tok_dev, 0)
        kept = lax.dynamic_slice_in_dim(own, sent, HALO, 0)
        return lax.dynamic_update_slice_in_dim(own, jnp.where(mine, kept, theirs), sent, 0)

    prm = grad_prm[:PROMPTS]
    if dp == 8:
        mid = width // 2
        lanes = lambda k: lax.dynamic_slice(prm, (0, k * mid), (PROMPTS, mid)).astype(bf16)
        part = lanes(core).astype(f32) + across(lanes(1 - core)).astype(f32)
        for turns in ((by_x, by_y, by_xy), tuple(functools.partial(by_z, bits=k) for k in (1, 2, 3))):
            sent_prm = part.astype(bf16)
            one, two, three = (turn(sent_prm).astype(f32) for turn in turns)
            part = (sent_prm.astype(f32) + one) + (two + three)
        part = (part / (row_count * dp)).astype(bf16)
        other = across(part)
        grad_prm = jnp.where(core == 0, jnp.concatenate([part, other], 1), jnp.concatenate([other, part], 1))
    else:
        grad_prm = (lax.psum(prm, ("dp", "tp")) / (row_count * dp)).astype(bf16)
    return (settle(output), settle(grad_tok), grad_prm)


def solution(mesh):
    return jax.shard_map(
        on_device,
        mesh=mesh,
        in_specs=(
            P(("dp", "tp"), None),
            P(),
            P("dp", None, "tp"),
            P("tp", "dp"),
            P("dp", "tp"),
            P("tp", "dp"),
            P(),
            P(),
            P("dp", None),
            P("dp", None),
            P(("dp", "tp"), None),
        ),
        out_specs=(P(("dp", "tp"), None), P(("dp", "tp"), None), P()),
        check_vma=False,
    )
```
